512 devices in a mesh: dp: 128 (over z, y, core), rep: 4 (over x).
Axes of the slice: x: 4, y: 8, z: 8, core: 2. Of those that a mesh axis runs over, the one named last changes fastest.
Arguments:
- tokens: bfloat16 [16384, 1664], P('dp'), may hold values from -6 to 6
- expert_ids: int32 [16384, 2], P('dp'), may hold values from 0 to 31, all different within a row; in each aligned block of 128 rows (0 to 127, 128 to 255, ...) at most 9 rows name the same one
- priority: int32 [16384], P('dp'), may hold values from 0 to 63
- gate_values: float32 [16384, 2], P('dp'), may hold values from 0.05 to 1
- weight_in: bfloat16 [128, 1664, 1024], P('dp', None, 'rep'), may hold values from -0.15625 to 0.15625
- weight_out: bfloat16 [128, 1024, 1664], P('dp', 'rep'), may hold values from -0.09375 to 0.09375
- cotangent: bfloat16 [16384, 1664], P('dp'), may hold values from -6 to 6
Outputs:
- output: bfloat16 [16384, 1664], P('dp', 'rep')
- grad_tokens: bfloat16 [16384, 1664], P('dp', 'rep')
- grad_gates: float32 [16384, 2], P(('dp', 'rep'))
- grad_weight_in: bfloat16 [128, 1664, 1024], P('dp', None, 'rep')
- grad_weight_out: bfloat16 [128, 1024, 1664], P('dp', 'rep')
The draws below stay inside these ranges and needn't reach their ends.
Inputs may be any that keep to these rules, and one draw needn't show every extreme that they name: `expert_ids`: the two ids of a token differ. Among the 128 tokens of one index of dp no expert is named more than 9 times, and 9 is reached.
All inputs are finite; a program needn't handle non-finite values.
Results may differ from the reference program's by a relative error of at most 0.017.
Values may be sent and summed in bfloat16 or wider, within the bound.
A program may use at most 128 MiB of HBM per device.

```python
import math
import jax
import jax.numpy as jnp
import numpy as np
from jax import lax

D = 1664
HID = 4096
HBLK = 4
PRIO = 64
TOK_DEV = 128
EXPERTS = 32
TOKENS = 16384
SLOT = 9
CAP = 1024
N_REP = 4


def with_ends(result, key, smallest, largest):
    spot = [jax.random.randint(jax.random.fold_in(key, axis), (), 0, length) for axis, length in enumerate(result.shape)]
    widest = result.shape.index(max(result.shape))
    beside = spot[:widest] + [(spot[widest] + 1) % result.shape[widest]] + spot[widest + 1:]
    return result.at[tuple(spot)].set(smallest).at[tuple(beside)].set(largest)


def block_scale(key, extent, pieces, least, top_value):
    loudness, own = 1.0, jax.random.fold_in(key, 6)
    for dim, blocks in pieces:
        steps = jnp.exp(jax.random.uniform(jax.random.fold_in(own, dim), (blocks,), jnp.float32, least / len(pieces), top_value / len(pieces)))
        loudness = loudness * jnp.repeat(steps, extent[dim] // blocks).reshape([-1 if axis == dim else 1 for axis in range(len(extent))])
    return loudness


def deal_out(rng, own, number, rows, amount, top, limit, skew):
    sequence = jax.random.permutation(rng, amount)
    packed, ordinary = portions_of(amount, rows * top, limit, skew, True), portions_of(amount, rows * top, limit, skew, False)
    places = jnp.arange(amount)

    def named(lengths, rotation):
        used = int((lengths > 0).sum())
        fixed = max(1, used // 4)
        passed = fixed + (places - fixed + rotation * (used - fixed)) % max(1, amount - fixed)
        return jnp.zeros((amount,), jnp.int32).at[sequence[jnp.where(places < fixed, places, passed)]].set(jnp.asarray(lengths, jnp.int32))

    lengths = jnp.where(number % 4 == 0, named(packed, number // 4), named(ordinary, number - number // 4 - 1))
    mixed = jax.random.permutation(jax.random.fold_in(own, 3), amount)
    source_of, receiver = mixed[0:amount // 2 * 2:2], mixed[1:amount // 2 * 2:2]
    slack = jnp.minimum(lengths[source_of] - 1, limit - lengths[receiver]) // 2
    slack = jnp.where((source_of == sequence[0]) | (receiver == sequence[0]) | (lengths[receiver] == 0), 0, jnp.maximum(slack, 0))
    passed = jax.random.randint(jax.random.fold_in(own, 4), (amount // 2,), 0, 1 << 20) % (slack + 1)
    lengths = lengths.at[source_of].add(-passed).at[receiver].add(passed)
    labels = jnp.searchsorted(jnp.cumsum(lengths), jnp.arange(rows * top), side="right").astype(jnp.int32)
    table = labels.reshape(top, rows).T
    table = table[jax.random.permutation(jax.random.fold_in(own, 1), rows)]
    rotation = jax.random.randint(jax.random.fold_in(own, 2), (rows, 1), 0, top)
    return jnp.take_along_axis(table, (jnp.arange(top)[None, :] + rotation) % top, axis=1)


def portions_of(count, total, bound, skew, full):
    portions = [(1 << 20) // math.isqrt(standing ** skew) + 1 for standing in range(1, count + 1)]
    largest = bound if full else min(bound, max(-(-total // count), total * portions[0] // sum(portions)))
    least = 1 if total - largest >= count - 1 else 0
    given, rest = [largest] + [least] * (count - 1), total - largest - least * (count - 1)
    while rest > 0:
        movable = [i for i in range(1, count) if given[i] < largest] or [i for i in range(1, count) if given[i] < bound]
        whole, budget = sum([portions[i] for i in movable]), rest
        for i in movable:
            addition = min(bound - given[i], max(1, budget * portions[i] // whole), rest)
            given[i] = given[i] + addition
            rest = rest - addition
    return np.array(given)


def normal_values(stream_key, dims, scale, limit, cuts=(), kind=jnp.bfloat16):
    entries = jax.random.normal(stream_key, dims, jnp.float32) * scale
    if len(cuts) > 0:
        entries = block_scale(stream_key, dims, cuts, -0.22, 0.18) * entries
    return jnp.clip(entries, min=-limit, max=limit).astype(kind)


def setup_inputs(seed: int = 0) -> dict:
    arg_keys = jax.random.split(jax.random.key(seed), 8)
    tokens = normal_values(arg_keys[0], (TOKENS, D), 1.0, 6.0, ((0, 128),))
    expert_ids_keys = jax.random.split(jax.random.fold_in(arg_keys[1], 1), TOKENS // TOK_DEV)
    expert_ids_turns = jax.random.permutation(jax.random.fold_in(arg_keys[1], 3), TOKENS // TOK_DEV)
    expert_ids = jax.vmap(lambda own, number: deal_out(jax.random.fold_in(arg_keys[1], 2), own, number, TOK_DEV, EXPERTS, 2, SLOT, 2))(expert_ids_keys, expert_ids_turns).reshape((TOKENS, 2))
    priority = with_ends(jax.random.randint(arg_keys[2], (TOKENS,), 0, PRIO), jax.random.fold_in(arg_keys[2], 1), 0, PRIO - 1).astype(jnp.int32)
    gate_values = jnp.clip(0.05 + 0.95 * jax.random.uniform(arg_keys[3], (TOKENS, 2), jnp.float32) ** block_scale(arg_keys[3], (TOKENS, 2), ((0, 128),), -0.2, 0.2), 0.05, 1.0)
    weight_in = normal_values(arg_keys[4], (HBLK * EXPERTS, D, HID // HBLK), D ** -0.5, 0.15625, ((0, 128), (2, 4)))
    weight_out = normal_values(arg_keys[5], (HBLK * EXPERTS, HID // HBLK, D), HID ** -0.5, 0.09375, ((0, 128), (1, 4)))
    cotangent = normal_values(arg_keys[6], (TOKENS, D), 1.0, 6.0, ((0, 128),))
    return {"tokens": tokens, "expert_ids": expert_ids, "priority": priority, "gate_values": gate_values, "weight_in": weight_in, "weight_out": weight_out, "cotangent": cotangent}


def gelu_parts(hidden_pre):
    normal_cdf = 0.5 * (1.0 + jax.scipy.special.erf(hidden_pre * (1.0 / math.sqrt(2.0))))
    density = jnp.exp(-0.5 * hidden_pre * hidden_pre) * (1.0 / math.sqrt(2.0 * math.pi))
    return (hidden_pre * normal_cdf, normal_cdf + hidden_pre * density)

def reference(tokens, expert_ids, priority, gate_values, weight_in, weight_out, cotangent):
    token_count = tokens.shape[0]
    model_width = tokens.shape[1]
    blocks = HBLK * N_REP
    block_width = HID // blocks
    assignments = 2 * token_count
    priority_key = (priority[:, None] + PRIO * (1 - jnp.arange(2, dtype=jnp.int32))[None, :]).reshape(-1)
    flat_expert = expert_ids.reshape(-1)
    expert_hot = (flat_expert[:, None] == jnp.arange(EXPERTS, dtype=jnp.int32)[None, :]).astype(jnp.int32)
    key_hot = (priority_key[:, None] == jnp.arange(2 * PRIO, dtype=jnp.int32)[None, :]).astype(jnp.int32)
    counts = jnp.dot(expert_hot.T, key_hot, preferred_element_type=jnp.int32)
    above_count = jnp.cumsum(counts[:, ::-1], axis=1)[:, ::-1]
    cutoff_key = lax.optimization_barrier(jnp.sum((above_count > CAP).astype(jnp.int32), axis=1))
    kept_mask = priority_key >= lax.optimization_barrier(jnp.sum(expert_hot * cutoff_key[None, :], axis=1))
    kept_hot = expert_hot * kept_mask.astype(jnp.int32)[:, None]
    position = lax.optimization_barrier(jnp.sum(kept_hot * (jnp.cumsum(kept_hot, axis=0) - kept_hot), axis=1))
    target = jnp.where(kept_mask, flat_expert * CAP + position, EXPERTS * CAP).astype(jnp.int32)
    table = jnp.full((EXPERTS * CAP + 1,), assignments, jnp.int32)
    table = table.at[target].set(jnp.arange(assignments, dtype=jnp.int32))
    members_all = table[:EXPERTS * CAP]
    in_full = weight_in.reshape(EXPERTS, HBLK, model_width, HID // HBLK).transpose(0, 2, 1, 3).reshape(EXPERTS, model_width, HID)
    out_full = weight_out.reshape(EXPERTS, HID, model_width)
    flat_gate = gate_values.reshape(-1)

    def one_expert(operands):
        members, matrix_in, matrix_out = operands
        valid = members < assignments
        safe_index = jnp.where(valid, members, 0)
        token_id = safe_index // 2
        rows = jnp.where(valid[:, None], tokens[token_id], jnp.zeros((), tokens.dtype))
        scale = jnp.where(valid, flat_gate[safe_index], jnp.zeros((), flat_gate.dtype))
        grad_rows = (scale[:, None] * cotangent[token_id].astype(jnp.float32)).astype(jnp.bfloat16)
        hidden_pre = jnp.dot(rows, matrix_in, preferred_element_type=jnp.float32)
        activation, slope = gelu_parts(hidden_pre)
        activation = activation.astype(jnp.bfloat16)
        partial_out = jnp.einsum('rbh,bhd->rbd', activation.reshape(CAP, blocks, block_width).astype(jnp.float32), matrix_out.reshape(blocks, block_width, model_width).astype(jnp.float32)).astype(jnp.bfloat16)
        expert_out = lax.optimization_barrier(jnp.sum(partial_out.astype(jnp.float32), axis=1))
        grad_act = jnp.dot(grad_rows, matrix_out.T, preferred_element_type=jnp.float32)
        grad_pre = (grad_act * slope).astype(jnp.bfloat16)
        grad_in = jnp.dot(rows.T, grad_pre, preferred_element_type=jnp.float32).astype(jnp.bfloat16)
        grad_out = jnp.dot(activation.T, grad_rows, preferred_element_type=jnp.float32).astype(jnp.bfloat16)
        partial_dx = jnp.einsum('rbh,dbh->rbd', grad_pre.reshape(CAP, blocks, block_width).astype(jnp.float32), matrix_in.reshape(model_width, blocks, block_width).astype(jnp.float32)).astype(jnp.bfloat16)
        expert_dx = lax.optimization_barrier(jnp.sum(partial_dx.astype(jnp.float32), axis=1))
        return (expert_out, expert_dx, grad_in, grad_out)
    expert_out, expert_dx, grad_in, grad_out = lax.map(one_expert, (members_all.reshape(EXPERTS, CAP), in_full, out_full))
    out_rows = jnp.zeros((assignments + 1, model_width), jnp.float32)
    out_rows = out_rows.at[members_all].set(expert_out.reshape(-1, model_width))
    out_rows = out_rows[:assignments].reshape(token_count, 2, model_width)
    dx_rows = jnp.zeros((assignments + 1, model_width), jnp.float32)
    dx_rows = dx_rows.at[members_all].set(expert_dx.reshape(-1, model_width))
    dx_rows = dx_rows[:assignments].reshape(token_count, 2, model_width)
    output = lax.optimization_barrier(jnp.sum(gate_values[:, :, None] * out_rows, axis=1)).astype(jnp.bfloat16)
    grad_tokens = lax.optimization_barrier(jnp.sum(dx_rows, axis=1)).astype(jnp.bfloat16)
    grad_gates = lax.optimization_barrier(jnp.sum(cotangent.astype(jnp.float32)[:, None, :] * out_rows, axis=2))
    grad_weight_in = grad_in.reshape(EXPERTS, model_width, HBLK, HID // HBLK).transpose(0, 2, 1, 3).reshape(EXPERTS * HBLK, model_width, HID // HBLK)
    grad_weight_out = grad_out.reshape(EXPERTS * HBLK, HID // HBLK, model_width)
    return (output, grad_tokens, grad_gates, grad_weight_in, grad_weight_out)
```

```python
import functools
import math

import jax
import jax.numpy as jnp
import numpy as np
from jax import lax
from jax.experimental import pallas as pl
from jax.experimental.pallas import tpu as pltpu
from jax.sharding import PartitionSpec as P

MESH = pl.DeviceIdType.MESH
D = 1664
NZ = 8
SLOTS = 9
PAD = 16
ROWS = 80
GROUP = 16
WIDE = 2 * D + 128
PRIO = 64
CAP = 1024
HID = 256
BF = jnp.bfloat16
F32 = jnp.float32
VMEM_LIMIT = 56 * 1024 * 1024


def place():
    dp = lax.axis_index("dp")
    x = lax.axis_index("rep")
    z = dp // 16
    y = (dp // 2) % 8
    return dp, x, z, y // 2, y % 2, dp % 2


def compact_matrix():
    m = np.zeros((ROWS, NZ * PAD), np.float32)
    for src in range(NZ):
        for slot in range(SLOTS):
            m[src * SLOTS + slot, src * PAD + slot] = 1.0
    return m


def dot(a, b, dims=(((1,), (0,)), ((), ()))):
    return lax.dot_general(a, b, dims, preferred_element_type=F32)


def prepare_kernel(ids_ref, prio_ref, gate_ref, tok_ref, cot_ref, send_ref, m0_ref, m1_ref):
    _, x, _, ps, _, _ = place()
    lane = lax.broadcasted_iota(jnp.int32, (128, 128), 1)
    row = lax.broadcasted_iota(jnp.int32, (128, 128), 0)
    ids = [ids_ref[:, k : k + 1] for k in range(2)]
    hot = [(ids[k] == lane).astype(F32) for k in range(2)]
    lower = (lane < row).astype(BF)
    before = dot(lower, (hot[0] + hot[1]).astype(BF))
    picks = []
    for k in range(2):
        slot = jnp.sum(hot[k] * before, axis=1, keepdims=True).astype(jnp.int32)
        ze = lax.shift_right_logical(ids[k], 2)
        pe = lax.bitwise_and(ids[k], 3)
        mine = lax.bitwise_and(ps + pe + ze, 3) == x
        position = jnp.where(mine, ze * PAD + slot, -1)
        picks.append((position == lane).astype(F32))
    m0_ref[...] = picks[0].astype(BF)
    m1_ref[...] = picks[1].astype(BF)
    turned = [p.T.astype(BF) for p in picks]
    both = turned[0] + turned[1]
    cot = cot_ref[...].astype(F32)
    weighted = [(gate_ref[:, k : k + 1] * cot).astype(BF) for k in range(2)]
    rows = dot(both, tok_ref[...]).astype(BF)
    grads = (dot(turned[0], weighted[0]) + dot(turned[1], weighted[1])).astype(BF)
    key = prio_ref[...] + 1
    keys = [jnp.broadcast_to((key + PRIO * (1 - k)).astype(F32), (128, 128)).astype(BF) for k in range(2)]
    key_rows = (dot(turned[0], keys[0]) + dot(turned[1], keys[1])).astype(BF)
    send_ref[:, :, 0:D] = rows.reshape(NZ, PAD, D)
    send_ref[:, :, D : 2 * D] = grads.reshape(NZ, PAD, D)
    send_ref[:, :, 2 * D : WIDE] = key_rows.reshape(NZ, PAD, 128)


def prepare(ids, prio, gates, tokens, cotangent):
    return pl.pallas_call(
        prepare_kernel,
        out_shape=(
            jax.ShapeDtypeStruct((NZ, PAD, WIDE), BF),
            jax.ShapeDtypeStruct((128, 128), BF),
            jax.ShapeDtypeStruct((128, 128), BF),
        ),
        in_specs=[pl.BlockSpec(memory_space=pltpu.VMEM)] * 5,
        out_specs=[pl.BlockSpec(memory_space=pltpu.VMEM)] * 3,
        compiler_params=pltpu.CompilerParams(vmem_limit_bytes=VMEM_LIMIT),
        name="prepare",
    )(ids, prio, gates, tokens, cotangent)


def partners():
    dp, x, z, pair, _, _ = place()
    own = (x + 16 - 2 * pair - z) % 4 == 0
    targets, sources, steps = [], [], []
    for r in range(NZ):
        j = (z + r) % NZ
        targets.append((j * 4 + (x + 16 - pair - j) % 4) * 4 + dp % 4)
        sources.append((j * 4 + (x + 16 - pair - z) % 4) * 4 + dp % 4)
        steps.append(j)
    return own, targets, sources, steps


def neighbours():
    dp, x, _, _, yp, c = place()
    return (dp + 1 - 2 * c, x), (dp + 2 - 4 * yp, x), (dp, (x + 1) % 4), (dp, (x + 3) % 4), (dp, (x + 2) % 4)


def greet(own, targets, sources, near):
    barrier = pltpu.get_barrier_semaphore()
    _, x, _, _, _, _ = place()

    def tell(device):
        pl.semaphore_signal(barrier, inc=1, device_id=device, device_id_type=MESH)

    for device in near:
        tell(device)
    for r in range(1, NZ):
        tell((targets[r], x))
        if r != NZ // 2:
            tell((sources[r], x))

    @pl.when(jnp.logical_not(own))
    def _():
        tell((targets[0], x))

    count = len(near) + 2 * (NZ - 1) - 1
    pl.semaphore_wait(barrier, jnp.where(own, count, count + 1))


def exchange(own, peers, steps, index, src, dst, send, recv, x):
    for r in range(1, NZ):
        pltpu.make_async_remote_copy(
            src_ref=src.at[steps[r]], dst_ref=dst.at[index], send_sem=send.at[r], recv_sem=recv.at[index],
            device_id=(peers[r], x), device_id_type=MESH,
        ).start()

    @pl.when(own)
    def _():
        copy = pltpu.make_async_copy(src.at[steps[0]], dst.at[index], send.at[0])
        copy.start()
        copy.wait()

    @pl.when(jnp.logical_not(own))
    def _():
        pltpu.make_async_remote_copy(
            src_ref=src.at[steps[0]], dst_ref=dst.at[index], send_sem=send.at[0], recv_sem=recv.at[index],
            device_id=(peers[0], x), device_id_type=MESH,
        ).start()


def exchange_wait(own, peers, steps, src, dst, send, recv, x, side):
    def handle(r):
        return pltpu.make_async_remote_copy(
            src_ref=src.at[steps[r]], dst_ref=dst.at[steps[r]], send_sem=send.at[r], recv_sem=recv.at[steps[r]],
            device_id=(peers[r], x), device_id_type=MESH,
        )

    def wait(r):
        if side == "recv":
            handle(r).wait_recv()
        else:
            handle(r).wait_send()

    for r in range(1, NZ):
        wait(r)

    @pl.when(jnp.logical_not(own))
    def _():
        wait(0)


def dispatch_kernel(send_ref, compact_ref, rows_ref, landing, send_a, recv_a, send_b, recv_b, recv_h):
    dp, x, z, pair, yp, c = place()
    own, targets, sources, steps = partners()
    sibling, across, right, left, _ = neighbours()
    greet(own, targets, sources, (sibling, across, right, left))
    exchange(own, targets, steps, z, send_ref, landing, send_a, recv_a, x)
    exchange_wait(own, sources, steps, send_ref, landing, send_a, recv_a, x, "recv")

    def block(xx, yy):
        return c * 8 + yy * 4 + xx

    mine = block(x, yp)
    for lo in range(0, WIDE, 1152):
        part = landing[:, :, lo : lo + 1152].reshape(NZ * PAD, 1152)
        rows_ref[mine, :, lo : lo + 1152] = dot(compact_ref[...], part).astype(BF)

    started = []

    def send(src, sem, target):
        copy = pltpu.make_async_remote_copy(
            src_ref=src, dst_ref=src, send_sem=send_b.at[len(started)], recv_sem=sem, device_id=target, device_id_type=MESH
        )
        copy.start()
        started.append(copy)

    def whole(b, target):
        send(rows_ref.at[b], recv_b.at[b], target)

    half = (slice(0, 1792), slice(1792, WIDE))

    def arrived(b):
        pltpu.make_async_remote_copy(
            src_ref=rows_ref.at[b], dst_ref=rows_ref.at[b], send_sem=send_b.at[0], recv_sem=recv_b.at[b],
            device_id=sibling, device_id_type=MESH,
        ).wait_recv()

    whole(mine, right)
    whole(mine, left)
    whole(mine, across)
    whole(mine, sibling)
    other = block(x, 1 - yp)
    arrived(other)
    whole(other, right)
    whole(other, left)
    whole(other, sibling)
    xl, xr, xo = (x + 3) % 4, (x + 1) % 4, (x + 2) % 4
    for n, yy in enumerate((yp, 1 - yp)):
        b = block(xl, yy)
        arrived(b)
        send(rows_ref.at[b, :, half[0]], recv_h.at[2 * yy], right)
        whole(b, sibling)
        b = block(xr, yy)
        arrived(b)
        send(rows_ref.at[b, :, half[1]], recv_h.at[2 * yy + 1], left)
        whole(b, sibling)
    for yy in (yp, 1 - yp):
        b = block(xo, yy)
        for h in range(2):
            part = rows_ref.at[b, :, half[h]]
            pltpu.make_async_remote_copy(
                src_ref=part, dst_ref=part, send_sem=send_b.at[0], recv_sem=recv_h.at[2 * yy + h],
                device_id=sibling, device_id_type=MESH,
            ).wait_recv()
        whole(b, sibling)
    for i in range(8):
        arrived((1 - c) * 8 + i)
    for copy in started:
        copy.wait_send()
    exchange_wait(own, targets, steps, send_ref, landing, send_a, recv_a, x, "send")


def dispatch(send, compact):
    return pl.pallas_call(
        dispatch_kernel,
        out_shape=jax.ShapeDtypeStruct((GROUP, ROWS, WIDE), BF),
        in_specs=[pl.BlockSpec(memory_space=pltpu.VMEM)] * 2,
        out_specs=pl.BlockSpec(memory_space=pltpu.VMEM),
        scratch_shapes=[
            pltpu.VMEM((NZ, PAD, WIDE), BF),
            pltpu.SemaphoreType.DMA((NZ,)),
            pltpu.SemaphoreType.DMA((NZ,)),
            pltpu.SemaphoreType.DMA((17,)),
            pltpu.SemaphoreType.DMA((16,)),
            pltpu.SemaphoreType.DMA((4,)),
        ],
        compiler_params=pltpu.CompilerParams(collective_id=0, has_side_effects=True, vmem_limit_bytes=VMEM_LIMIT),
        name="dispatch",
    )(send, compact)


def experts_kernel(rows_ref, keys_ref, win_ref, wout_ref, part_ref, gin_ref, gout_ref, acc_in, acc_out, cut_ref):
    step = pl.program_id(0)

    @pl.when(step == 0)
    def _():
        lane = lax.broadcasted_iota(jnp.int32, (GROUP * ROWS, 128), 1).astype(F32)
        above = jnp.sum((keys_ref[...].astype(F32) > lane).astype(F32), axis=0, keepdims=True)
        cutoff = jnp.sum((above > CAP).astype(F32), axis=1, keepdims=True)
        cut_ref[...] = jnp.broadcast_to(cutoff, (8, 128))
        acc_in[...] = jnp.zeros_like(acc_in)
        acc_out[...] = jnp.zeros_like(acc_out)

    last = (((1,), (1,)), ((), ()))
    first = (((0,), (0,)), ((), ()))
    tok = rows_ref[:, 0:D]
    grad = rows_ref[:, D : 2 * D]
    keep = (rows_ref[:, 2 * D : 2 * D + 1].astype(F32) > cut_ref[0:1, 0:1]).astype(F32)
    win = win_ref[...]
    wout = wout_ref[...]
    pre = dot(tok, win)
    cdf = 0.5 * (1.0 + lax.erf(pre * (1.0 / math.sqrt(2.0))))
    density = jnp.exp(-0.5 * pre * pre) * (1.0 / math.sqrt(2.0 * math.pi))
    act = (pre * cdf * keep).astype(BF)
    gact = dot(grad, wout, last)
    gpre = (gact * (cdf + pre * density) * keep).astype(BF)
    part_ref[:, 0:D] = dot(act, wout).astype(BF)
    part_ref[:, D : 2 * D] = dot(gpre, win, last).astype(BF)
    acc_in[...] += dot(tok, gpre, first)
    acc_out[...] += dot(act, grad, first)

    @pl.when(step == pl.num_programs(0) - 1)
    def _():
        gin_ref[...] = acc_in[...].astype(BF)
        gout_ref[...] = acc_out[...].astype(BF)


def experts(rows, win, wout):
    tile = 256
    total = GROUP * ROWS
    return pl.pallas_call(
        experts_kernel,
        grid=(total // tile,),
        out_shape=(
            jax.ShapeDtypeStruct((total, 2 * D), BF),
            jax.ShapeDtypeStruct((D, HID), BF),
            jax.ShapeDtypeStruct((HID, D), BF),
        ),
        in_specs=[
            pl.BlockSpec((tile, WIDE), lambda i: (i, 0)),
            pl.BlockSpec((total, 128), lambda i: (0, 2 * D // 128)),
            pl.BlockSpec((D, HID), lambda i: (0, 0)),
            pl.BlockSpec((HID, D), lambda i: (0, 0)),
        ],
        out_specs=[
            pl.BlockSpec((tile, 2 * D), lambda i: (i, 0)),
            pl.BlockSpec((D, HID), lambda i: (0, 0)),
            pl.BlockSpec((HID, D), lambda i: (0, 0)),
        ],
        scratch_shapes=[pltpu.VMEM((D, HID), F32), pltpu.VMEM((HID, D), F32), pltpu.VMEM((8, 128), F32)],
        compiler_params=pltpu.CompilerParams(vmem_limit_bytes=VMEM_LIMIT),
        name="experts",
    )(rows, rows, win, wout)


def add(*parts):
    total = parts[0].astype(F32)
    for p in parts[1:]:
        total = total + p.astype(F32)
    return total.astype(BF)


def combine_kernel(
    part_ref, expand_ref, m0_ref, m1_ref, gate_ref, cot_ref, out_ref, dx_ref, gg_ref,
    tot, halves, full, ysum, yrecv, spread, back, chunk, chunk_in, gg, gg_in,
    send_c, recv_c, send_h, recv_h, send_f, recv_f, send_y, recv_y, send_e, recv_e, send_o, recv_o, send_g, recv_g,
):
    dp, x, z, pair, yp, c = place()
    own, targets, sources, steps = partners()
    sibling, across, right, left, far = neighbours()
    greet(own, targets, sources, (sibling, across, right, left, far))

    def remote(src, dst, ssem, rsem, target):
        return pltpu.make_async_remote_copy(
            src_ref=src, dst_ref=dst, send_sem=ssem, recv_sem=rsem, device_id=target, device_id_type=MESH
        )

    xl, xr, xo = (x + 3) % 4, (x + 1) % 4, (x + 2) % 4
    order = [(yy, xx) for yy in (1 - yp, yp) for xx in (xo, xr, xl, x)]

    def core_copy(yy, xx):
        i = yy * 4 + xx
        return remote(part_ref.at[(1 - c) * 8 + i], tot.at[i], send_c.at[i], recv_c.at[i], sibling)

    for yy, xx in order:
        core_copy(yy, xx).start()

    def merged(yy, xx):
        i = yy * 4 + xx
        core_copy(yy, xx).wait_recv()
        tot[i] = add(tot[i], part_ref[c * 8 + i])
        return i

    def half_copy(yy, h):
        part = tot.at[yy * 4 + xo, :, h * D : (h + 1) * D]
        k = 2 * yy + h
        return remote(part, halves.at[k], send_h.at[k], recv_h.at[k], right if h == 0 else left)

    def full_copy(yy, h):
        k = 2 * yy + h
        i = yy * 4 + (xr if h == 0 else xl)
        return remote(tot.at[i], full.at[k], send_f.at[k], recv_f.at[k], right if h == 0 else left)

    y_copy = remote(ysum, yrecv, send_y.at[0], recv_y.at[0], across)
    for yy in (1 - yp, yp):
        merged(yy, xo)
        half_copy(yy, 0).start()
        half_copy(yy, 1).start()
        merged(yy, xr)
        merged(yy, xl)
        merged(yy, x)
    for yy in (1 - yp, yp):
        for h in range(2):
            half_copy(yy, h).wait_recv()
            i = yy * 4 + (xr if h == 0 else xl)
            tot[i, :, h * D : (h + 1) * D] = add(tot[i, :, h * D : (h + 1) * D], halves[2 * yy + h])
            full_copy(yy, h).start()
    yy = 1 - yp
    full_copy(yy, 0).wait_recv()
    full_copy(yy, 1).wait_recv()
    ysum[...] = add(tot[yy * 4 + x], full[2 * yy], full[2 * yy + 1])
    y_copy.start()
    yy = yp
    full_copy(yy, 0).wait_recv()
    full_copy(yy, 1).wait_recv()
    y_copy.wait_recv()
    final = add(tot[yy * 4 + x], full[2 * yy], full[2 * yy + 1], yrecv[...])
    for lo in range(0, 2 * D, D):
        spread[:, :, lo : lo + D] = dot(expand_ref[...], final[:, lo : lo + D]).astype(BF).reshape(NZ, PAD, D)

    exchange(own, sources, steps, z, spread, back, send_e, recv_e, x)
    exchange_wait(own, targets, steps, spread, back, send_e, recv_e, x, "recv")

    m0 = m0_ref[...]
    m1 = m1_ref[...]
    rows = back[:, :, 0:D].reshape(NZ * PAD, D)
    picked0 = dot(m0, rows)
    picked1 = dot(m1, rows)
    cot = cot_ref[...].astype(F32)
    lane = lax.broadcasted_iota(jnp.int32, (128, 128), 1)
    gg0 = jnp.sum(cot * picked0, axis=1, keepdims=True)
    gg1 = jnp.sum(cot * picked1, axis=1, keepdims=True)
    gg[...] = jnp.where(lane == 0, gg0, jnp.where(lane == 1, gg1, 0.0)).reshape(4, 32, 128)
    mixed = gate_ref[:, 0:1] * picked0 + gate_ref[:, 1:2] * picked1
    moved = dot(m0 + m1, back[:, :, D : 2 * D].reshape(NZ * PAD, D))
    for i in range(4):
        chunk[i, 0] = mixed[:, i * 416 : (i + 1) * 416].astype(BF)
        chunk[i, 1] = moved[:, i * 416 : (i + 1) * 416].astype(BF)

    def last_copies(to, n):
        device = (dp, to)
        return (
            remote(chunk.at[to], chunk_in.at[n], send_o.at[n], recv_o.at[n], device),
            remote(gg.at[to], gg_in.at[n], send_g.at[n], recv_g.at[n], device),
        )

    tails = [c for n, to in enumerate((xo, xr, xl)) for c in last_copies(to, n)]
    for copy in tails:
        copy.start()
    for copy in tails:
        copy.wait_recv()
    sums = chunk[x].astype(F32)
    gates = gg[x]
    for n in range(3):
        sums = sums + chunk_in[n].astype(F32)
        gates = gates + gg_in[n]
    out_ref[...] = sums[0].astype(BF)
    dx_ref[...] = sums[1].astype(BF)
    gg_ref[...] = gates[:, 0:2]

    for yy, xx in order:
        core_copy(yy, xx).wait_send()
    for yy in (1 - yp, yp):
        for h in range(2):
            half_copy(yy, h).wait_send()
            full_copy(yy, h).wait_send()
    y_copy.wait_send()
    exchange_wait(own, sources, steps, spread, back, send_e, recv_e, x, "send")
    for copy in tails:
        copy.wait_send()


def combine(part, expand, m0, m1, gates, cotangent):
    dma = pltpu.SemaphoreType.DMA
    return pl.pallas_call(
        combine_kernel,
        out_shape=(
            jax.ShapeDtypeStruct((128, 416), BF),
            jax.ShapeDtypeStruct((128, 416), BF),
            jax.ShapeDtypeStruct((32, 2), F32),
        ),
        in_specs=[pl.BlockSpec(memory_space=pltpu.VMEM)] * 6,
        out_specs=[pl.BlockSpec(memory_space=pltpu.VMEM)] * 3,
        scratch_shapes=[
            pltpu.VMEM((8, ROWS, 2 * D), BF),
            pltpu.VMEM((4, ROWS, D), BF),
            pltpu.VMEM((4, ROWS, 2 * D), BF),
            pltpu.VMEM((ROWS, 2 * D), BF),
            pltpu.VMEM((ROWS, 2 * D), BF),
            pltpu.VMEM((NZ, PAD, 2 * D), BF),
            pltpu.VMEM((NZ, PAD, 2 * D), BF),
            pltpu.VMEM((4, 2, 128, 416), BF),
            pltpu.VMEM((3, 2, 128, 416), BF),
            pltpu.VMEM((4, 32, 128), F32),
            pltpu.VMEM((3, 32, 128), F32),
            dma((8,)), dma((8,)), dma((4,)), dma((4,)), dma((4,)), dma((4,)), dma((1,)), dma((1,)),
            dma((8,)), dma((8,)), dma((3,)), dma((3,)), dma((3,)), dma((3,)),
        ],
        compiler_params=pltpu.CompilerParams(collective_id=1, has_side_effects=True, vmem_limit_bytes=VMEM_LIMIT),
        name="combine",
    )(part, expand, m0, m1, gates, cotangent)


def body(tokens, expert_ids, priority, gate_values, weight_in, weight_out, cotangent):
    compact = compact_matrix()
    send, m0, m1 = prepare(expert_ids, priority[:, None], gate_values, tokens, cotangent)
    rows = dispatch(send, jnp.asarray(compact, BF))
    part, grad_in, grad_out = experts(rows.reshape(GROUP * ROWS, WIDE), weight_in[0], weight_out[0])
    mixed, token_grad, gate_grad = combine(
        part.reshape(GROUP, ROWS, 2 * D), jnp.asarray(compact.T, BF), m0, m1, gate_values, cotangent
    )
    return mixed, token_grad, gate_grad, grad_in[None], grad_out[None]


def solution(mesh):
    placed = (
        P("dp", None),
        P("dp", None),
        P("dp"),
        P("dp", None),
        P("dp", None, "rep"),
        P("dp", "rep", None),
        P("dp", None),
    )
    return jax.shard_map(
        body,
        mesh=mesh,
        in_specs=placed,
        out_specs=(
            P("dp", "rep"),
            P("dp", "rep"),
            P(("dp", "rep"), None),
            P("dp", None, "rep"),
            P("dp", "rep", None),
        ),
        check_vma=False,
    )
```

```python
import math

import jax
import jax.numpy as jnp
import numpy as np
from jax import lax
from jax.experimental import pallas as pl
from jax.experimental.pallas import tpu as pltpu
from jax.sharding import PartitionSpec as P

MESH = pl.DeviceIdType.MESH
D = 1664
NZ = 8
SLOTS = 9
PAD = 16
HROWS = 40
WIDE = 2 * D + 128
TWO = 2 * D
OUTW = 416
PRIO = 64
CAP = 1024
HID = 256
BF = jnp.bfloat16
F32 = jnp.float32
VMEM_LIMIT = 60 * 1024 * 1024
LAST = (((1,), (1,)), ((), ()))
FIRST = (((0,), (0,)), ((), ()))


def place():
    dp = lax.axis_index("dp")
    x = lax.axis_index("rep")
    z = dp // 16
    y = (dp // 2) % 8
    return dp, x, z, y // 2, y % 2, dp % 2


def compact_matrix():
    m = np.zeros((HROWS, 4 * PAD), np.float32)
    for src in range(4):
        for slot in range(SLOTS):
            m[src * SLOTS + slot, src * PAD + slot] = 1.0
    return m


def dot(a, b, dims=(((1,), (0,)), ((), ()))):
    return lax.dot_general(a, b, dims, preferred_element_type=F32)


def seat(r):
    return (r % 2) * 4 + r // 2


def remote(src, dst, ssem, rsem, device):
    return pltpu.make_async_remote_copy(
        src_ref=src, dst_ref=dst, send_sem=ssem, recv_sem=rsem, device_id=device, device_id_type=MESH
    )


def layer_kernel(
    ids_ref, prio_ref, gate_ref, tok_ref, cot_ref, win_ref, wout_ref, compact_ref, expand_ref,
    out_ref, dx_ref, gg_ref, gin_ref, gout_ref,
    sendbuf, landing, rows, part, tot, cross, halves, full, ysum, yrecv, spread, back, chunk, chunk_in, gg, gg_in,
    picks, gcol, act_all, gpre_all, keep_all,
    send_a, recv_a, send_b, recv_b, recv_h, send_c, recv_c, send_x, recv_x, send_hf, recv_hf,
    send_f, recv_f, send_y, recv_y, send_e, recv_e, send_o, recv_o, send_g, recv_g,
):
    dp, x, z, pair, yp, c = place()
    own = (x + 16 - 2 * pair - z) % 4 == 0
    sibling, across = (dp + 1 - 2 * c, x), (dp + 2 - 4 * yp, x)
    xl, xr, xo = (x + 3) % 4, (x + 1) % 4, (x + 2) % 4
    right, left, far = (dp, xr), (dp, xl), (dp, xo)
    targets, sources = [], []
    for r in range(NZ):
        j = (z + r) % NZ
        targets.append(((j * 4 + (x + 16 - pair - j) % 4) * 4 + dp % 4, x))
        sources.append(((j * 4 + (x + 16 - pair - z) % 4) * 4 + dp % 4, x))

    barrier = pltpu.get_barrier_semaphore()

    def tell(device):
        pl.semaphore_signal(barrier, inc=1, device_id=device, device_id_type=MESH)

    near = (sibling, across, right, left, far)
    for device in near:
        tell(device)
    for r in range(1, NZ):
        tell(targets[r])
        if r != NZ // 2:
            tell(sources[r])

    @pl.when(jnp.logical_not(own))
    def _():
        tell(targets[0])

    lane = lax.broadcasted_iota(jnp.int32, (128, 128), 1)
    row = lax.broadcasted_iota(jnp.int32, (128, 128), 0)
    ids = [ids_ref[k : k + 1, :] for k in range(2)]
    hot = [(row == ids[k]).astype(F32) for k in range(2)]
    before = dot((hot[0] + hot[1]).astype(BF), (row < lane).astype(BF))
    turned, gates_of, keys = [], [], []
    for k in range(2):
        slot = jnp.sum(hot[k] * before, axis=0, keepdims=True).astype(jnp.int32)
        ze = lax.shift_right_logical(ids[k], 2)
        pe = lax.bitwise_and(ids[k], 3)
        here = lax.bitwise_and(pair + pe + ze, 3) == x
        distance = lax.bitwise_and(ze + (8 - z), 7)
        position = jnp.where(here, distance * PAD + slot, -1)
        t = (row == position).astype(F32)
        turned.append(t.astype(BF))
        picks[k] = t.T.astype(BF)
        gate = gate_ref[k : k + 1, :]
        gates_of.append(jnp.sum(t * gate, axis=1, keepdims=True))
        gcol[k] = jnp.broadcast_to(gate, (128, 128)).T
        key = (prio_ref[...] + (1 + PRIO * (1 - k))).astype(F32)
        keys.append(jnp.sum(t * key, axis=1, keepdims=True))
    cot16 = cot_ref[...]
    placed = dot(turned[0] + turned[1], tok_ref[...]).astype(BF)
    grads = (gates_of[0] * dot(turned[0], cot16) + gates_of[1] * dot(turned[1], cot16)).astype(BF)
    sendbuf[:, :, 0:D] = placed.reshape(NZ, PAD, D)
    sendbuf[:, :, D:TWO] = grads.reshape(NZ, PAD, D)
    sendbuf[:, :, TWO:WIDE] = jnp.broadcast_to(keys[0] + keys[1], (128, 128)).astype(BF).reshape(NZ, PAD, 128)

    count = len(near) + 2 * (NZ - 1) - 1
    pl.semaphore_wait(barrier, jnp.where(own, count, count + 1))

    def out_copy(r):
        k = seat((NZ - r) % NZ)
        return remote(sendbuf.at[r], landing.at[k], send_a.at[r], recv_a.at[k], targets[r])

    def in_copy(r):
        k = seat(r)
        return remote(landing.at[k], landing.at[k], send_a.at[0], recv_a.at[k], sources[r])

    for r in (4, 2, 6):
        out_copy(r).start()

    @pl.when(jnp.logical_not(own))
    def _():
        out_copy(0).start()

    for r in (3, 5, 1, 7):
        out_copy(r).start()

    @pl.when(own)
    def _():
        copy = pltpu.make_async_copy(sendbuf.at[0], landing.at[0], send_a.at[0])
        copy.start()
        copy.wait()

    @pl.when(jnp.logical_not(own))
    def _():
        in_copy(0).wait_recv()

    started = []

    def send(src, rsem, device):
        copy = remote(src, src, send_b.at[len(started)], rsem, device)
        copy.start()
        started.append(copy)

    def block(xx, yy):
        return (yy * 4 + xx) * 2 + c

    def whole(b, h, device):
        send(rows.at[b, h], recv_b.at[2 * b + h], device)

    def arrived(b, h):
        remote(rows.at[b, h], rows.at[b, h], send_b.at[0], recv_b.at[2 * b + h], sibling).wait_recv()

    mine = block(x, yp)
    other = block(x, 1 - yp)
    cut = (slice(0, 1792), slice(1792, WIDE))
    for h in range(2):
        for r in (h, 2 + h, 4 + h, 6 + h):
            if r:
                in_copy(r).wait_recv()
        for lo in range(0, WIDE, 1152):
            got = landing[4 * h : 4 * h + 4, :, lo : lo + 1152].reshape(4 * PAD, 1152)
            rows[mine, h, :, lo : lo + 1152] = dot(compact_ref[...], got).astype(BF)
        for device in (across, right, left, sibling):
            whole(mine, h, device)
    for h in range(2):
        arrived(other, h)
        for device in (right, left, sibling):
            whole(other, h, device)

    win = win_ref[...]
    wout = wout_ref[...]

    def compute(yy, xx):
        u = yy * 4 + xx
        for h in range(2):
            arrived(2 * u + 1 - c, h)
        tok = rows[pl.ds(2 * u, 2), :, :, 0:D].reshape(4 * HROWS, D)
        grad = rows[pl.ds(2 * u, 2), :, :, D:TWO].reshape(4 * HROWS, D)
        pre = dot(tok, win)
        cdf = 0.5 * (1.0 + lax.erf(pre * (1.0 / math.sqrt(2.0))))
        density = jnp.exp(-0.5 * pre * pre) * (1.0 / math.sqrt(2.0 * math.pi))
        act = (pre * cdf).astype(BF)
        gpre = (dot(grad, wout, LAST) * (cdf + pre * density)).astype(BF)
        part[pl.ds(2 * u, 2), :, :, 0:D] = dot(act, wout).astype(BF).reshape(2, 2, HROWS, D)
        part[pl.ds(2 * u, 2), :, :, D:TWO] = dot(gpre, win, LAST).astype(BF).reshape(2, 2, HROWS, D)
        act_all[u] = act
        gpre_all[u] = gpre
        for h in range(2):
            core_copy(u, h).start()

    def core_copy(u, h):
        k = 2 * u + h
        return remote(part.at[2 * u + 1 - c, h], tot.at[u, h], send_c.at[k], recv_c.at[k], sibling)

    for h in range(2):
        b = block(xl, yp)
        arrived(b, h)
        send(rows.at[b, h, :, cut[0]], recv_h.at[2 * h], right)
        whole(b, h, sibling)
        b = block(xr, yp)
        arrived(b, h)
        send(rows.at[b, h, :, cut[1]], recv_h.at[2 * h + 1], left)
        whole(b, h, sibling)
    compute(yp, x)
    compute(1 - yp, x)
    for h in range(2):
        b = block(xo, yp)
        for s in range(2):
            piece = rows.at[b, h, :, cut[s]]
            remote(piece, piece, send_b.at[0], recv_h.at[2 * h + s], sibling).wait_recv()
        whole(b, h, across)
        whole(b, h, sibling)
    compute(yp, xl)
    compute(yp, xr)
    for h in range(2):
        for xx in (xl, xr):
            b = block(xx, 1 - yp)
            arrived(b, h)
            whole(b, h, sibling)
    compute(yp, xo)
    compute(1 - yp, xr)
    compute(1 - yp, xl)
    for h in range(2):
        b = block(xo, 1 - yp)
        arrived(b, h)
        whole(b, h, sibling)
    compute(1 - yp, xo)

    def merge(yy, xx, h):
        u = yy * 4 + xx
        core_copy(u, h).wait_recv()
        tot[u, h] = tot[u, h] + part[2 * u + c, h]

    def cross_copy(h):
        return remote(tot.at[(1 - yp) * 4 + xo, h], cross.at[h], send_x.at[h], recv_x.at[h], across)

    def half_copy(s, h):
        piece = tot.at[yp * 4 + xo, h, :, s * D : (s + 1) * D]
        k = 2 * s + h
        return remote(piece, halves.at[k], send_hf.at[k], recv_hf.at[k], right if s == 0 else left)

    def full_copy(o, s, h):
        u = (yp if o == 0 else 1 - yp) * 4 + (xr if s == 0 else xl)
        k = (2 * o + s) * 2 + h
        return remote(tot.at[u, h], full.at[k], send_f.at[k], recv_f.at[k], right if s == 0 else left)

    def y_copy(h):
        return remote(ysum.at[h], yrecv.at[h], send_y.at[h], recv_y.at[h], across)

    for h in range(2):
        merge(1 - yp, xr, h)
        full_copy(1, 0, h).start()
        merge(1 - yp, xl, h)
        full_copy(1, 1, h).start()
    for h in range(2):
        merge(1 - yp, xo, h)
        cross_copy(h).start()
    for h in range(2):
        merge(yp, xo, h)
        merge(yp, xr, h)
        merge(yp, xl, h)
        merge(yp, x, h)
        merge(1 - yp, x, h)

    level = lane[0:1, :].astype(F32)
    above = jnp.zeros((1, 128), F32)
    for u in range(8):
        key = rows[2 * u : 2 * u + 2, :, :, TWO:WIDE].reshape(4 * HROWS, 128).astype(F32)
        above = above + jnp.sum((key > level).astype(F32), axis=0, keepdims=True)
    cutoff = jnp.sum((above > CAP).astype(F32), axis=1, keepdims=True)
    for u in range(8):
        key = rows[2 * u : 2 * u + 2, :, :, TWO:WIDE].reshape(4 * HROWS, 128).astype(F32)
        keep_all[u] = (key > cutoff).astype(BF)
    keep_own = [(rows[mine, h, :, TWO : TWO + 1].astype(F32) > cutoff).astype(F32) for h in range(2)]

    for h in range(2):
        cross_copy(h).wait_recv()
        tot[yp * 4 + xo, h] = tot[yp * 4 + xo, h] + cross[h]
        half_copy(0, h).start()
        half_copy(1, h).start()

    for u in range(8):
        keep = jnp.concatenate([keep_all[u], keep_all[u]], axis=1)
        act_all[u] = act_all[u] * keep
        gpre_all[u] = gpre_all[u] * keep
    act_turned = act_all[...].reshape(32 * HROWS, HID)

    for h in range(2):
        full_copy(1, 0, h).wait_recv()
        full_copy(1, 1, h).wait_recv()
        total = tot[(1 - yp) * 4 + x, h].astype(F32) + full[4 + h].astype(F32) + full[6 + h].astype(F32)
        ysum[h] = total.astype(BF)
        y_copy(h).start()

    @pl.loop(0, 13)
    def _(i):
        at = pl.multiple_of(i * 128, 128)
        g = rows[:, :, :, pl.ds(D + at, 128)].reshape(32 * HROWS, 128)
        gout_ref[:, pl.ds(at, 128)] = dot(act_turned, g, FIRST).astype(BF)

    for h in range(2):
        for s in range(2):
            half_copy(s, h).wait_recv()
            u = yp * 4 + (xr if s == 0 else xl)
            lanes = slice(s * D, (s + 1) * D)
            tot[u, h, :, lanes] = tot[u, h, :, lanes] + halves[2 * s + h]
            full_copy(0, s, h).start()

    gpre_flat = gpre_all[...].reshape(32 * HROWS, HID)

    @pl.loop(0, 13)
    def _(i):
        at = pl.multiple_of(i * 128, 128)
        t = rows[:, :, :, pl.ds(at, 128)].reshape(32 * HROWS, 128)
        gin_ref[pl.ds(at, 128), :] = dot(t, gpre_flat, FIRST).astype(BF)

    def home_copy(r):
        k = (NZ - r) % NZ
        return remote(spread.at[seat(r)], back.at[k], send_e.at[r], recv_e.at[k], sources[r])

    def home_wait(r):
        remote(back.at[r], back.at[r], send_e.at[0], recv_e.at[r], targets[r]).wait_recv()

    for h in range(2):
        y_copy(h).wait_recv()
        total = tot[yp * 4 + x, h].astype(F32) + yrecv[h].astype(F32)
        for s in range(2):
            full_copy(0, s, h).wait_recv()
            total = total + full[2 * s + h].astype(F32)
        final = (total * keep_own[h]).astype(BF)
        for lo in (0, D):
            wide = dot(expand_ref[...], final[:, lo : lo + D]).astype(BF)
            spread[4 * h : 4 * h + 4, :, lo : lo + D] = wide.reshape(4, PAD, D)
        for r in (4 + h, 2 + h, 6 + h):
            home_copy(r).start()
        if h:
            home_copy(1).start()
        else:

            @pl.when(jnp.logical_not(own))
            def _():
                home_copy(0).start()

            @pl.when(own)
            def _():
                copy = pltpu.make_async_copy(spread.at[0], back.at[0], send_e.at[0])
                copy.start()
                copy.wait()

    for r in range(1, NZ):
        home_wait(r)

    @pl.when(jnp.logical_not(own))
    def _():
        home_wait(0)

    def tail(src, dst, ssem, rsem):
        return [remote(src(to), dst(n), ssem.at[n], rsem.at[n], (dp, to)) for n, to in enumerate((xo, xr, xl))]

    result = back[:, :, 0:D].reshape(NZ * PAD, D)
    picked0 = dot(picks[0], result)
    picked1 = dot(picks[1], result)
    mixed = gcol[0][:, 0:1] * picked0 + gcol[1][:, 0:1] * picked1
    for i in range(4):
        chunk[0, i] = mixed[:, i * OUTW : (i + 1) * OUTW].astype(BF)
    tails = tail(lambda to: chunk.at[0, to], lambda n: chunk_in.at[0, n], send_o.at[0], recv_o.at[0])
    for copy in tails:
        copy.start()
    moved = dot(picks[0] + picks[1], back[:, :, D:TWO].reshape(NZ * PAD, D))
    for i in range(4):
        chunk[1, i] = moved[:, i * OUTW : (i + 1) * OUTW].astype(BF)
    more = tail(lambda to: chunk.at[1, to], lambda n: chunk_in.at[1, n], send_o.at[1], recv_o.at[1])
    for copy in more:
        copy.start()
    cot = cot16.astype(F32)
    gg0 = jnp.sum(cot * picked0, axis=1, keepdims=True)
    gg1 = jnp.sum(cot * picked1, axis=1, keepdims=True)
    gg[...] = jnp.where(lane == 0, gg0, jnp.where(lane == 1, gg1, 0.0)).reshape(4, 32, 128)
    last = tail(lambda to: gg.at[to], lambda n: gg_in.at[n], send_g, recv_g)
    for copy in last:
        copy.start()
    tails = tails + more + last
    for copy in tails:
        copy.wait_recv()
    gates = gg[x]
    for n in range(3):
        gates = gates + gg_in[n]
    gg_ref[...] = gates[:, 0:2]
    for k, ref in enumerate((out_ref, dx_ref)):
        total = chunk[k, x].astype(F32)
        for n in range(3):
            total = total + chunk_in[k, n].astype(F32)
        ref[...] = total.astype(BF)

    for r in range(1, NZ):
        out_copy(r).wait_send()
        home_copy(r).wait_send()

    @pl.when(jnp.logical_not(own))
    def _():
        out_copy(0).wait_send()
        home_copy(0).wait_send()

    for copy in started + tails:
        copy.wait_send()
    for u in range(8):
        for h in range(2):
            core_copy(u, h).wait_send()
    for h in range(2):
        cross_copy(h).wait_send()
        y_copy(h).wait_send()
        for s in range(2):
            half_copy(s, h).wait_send()
            full_copy(0, s, h).wait_send()
            full_copy(1, s, h).wait_send()


def layer(*args):
    dma = pltpu.SemaphoreType.DMA
    vmem = pltpu.VMEM
    return pl.pallas_call(
        layer_kernel,
        out_shape=(
            jax.ShapeDtypeStruct((128, OUTW), BF),
            jax.ShapeDtypeStruct((128, OUTW), BF),
            jax.ShapeDtypeStruct((32, 2), F32),
            jax.ShapeDtypeStruct((D, HID), BF),
            jax.ShapeDtypeStruct((HID, D), BF),
        ),
        in_specs=[pl.BlockSpec(memory_space=vmem)] * 9,
        out_specs=[pl.BlockSpec(memory_space=vmem)] * 5,
        scratch_shapes=[
            vmem((NZ, PAD, WIDE), BF),
            vmem((NZ, PAD, WIDE), BF),
            vmem((16, 2, HROWS, WIDE), BF),
            vmem((16, 2, HROWS, TWO), BF),
            vmem((8, 2, HROWS, TWO), BF),
            vmem((2, HROWS, TWO), BF),
            vmem((4, HROWS, D), BF),
            vmem((8, HROWS, TWO), BF),
            vmem((2, HROWS, TWO), BF),
            vmem((2, HROWS, TWO), BF),
            vmem((NZ, PAD, TWO), BF),
            vmem((NZ, PAD, TWO), BF),
            vmem((2, 4, 128, OUTW), BF),
            vmem((2, 3, 128, OUTW), BF),
            vmem((4, 32, 128), F32),
            vmem((3, 32, 128), F32),
            vmem((2, 128, 128), BF),
            vmem((2, 128, 128), F32),
            vmem((8, 4 * HROWS, HID), BF),
            vmem((8, 4 * HROWS, HID), BF),
            vmem((8, 4 * HROWS, 128), BF),
            dma((8,)), dma((8,)), dma((32,)), dma((32,)), dma((4,)),
            dma((16,)), dma((16,)), dma((2,)), dma((2,)), dma((4,)), dma((4,)),
            dma((8,)), dma((8,)), dma((2,)), dma((2,)), dma((8,)), dma((8,)),
            dma((2, 3)), dma((2, 3)), dma((3,)), dma((3,)),
        ],
        compiler_params=pltpu.CompilerParams(collective_id=0, has_side_effects=True, vmem_limit_bytes=VMEM_LIMIT),
        name="layer",
    )(*args)


def body(tokens, expert_ids, priority, gate_values, weight_in, weight_out, cotangent):
    compact = compact_matrix()
    mixed, token_grad, gate_grad, grad_in, grad_out = layer(
        expert_ids.T, priority[None, :], gate_values.T, tokens, cotangent, weight_in[0], weight_out[0],
        jnp.asarray(compact, BF), jnp.asarray(compact.T, BF),
    )
    return mixed, token_grad, gate_grad, grad_in[None], grad_out[None]


def solution(mesh):
    placed = (
        P("dp", None),
        P("dp", None),
        P("dp"),
        P("dp", None),
        P("dp", None, "rep"),
        P("dp", "rep", None),
        P("dp", None),
    )
    return jax.shard_map(
        body,
        mesh=mesh,
        in_specs=placed,
        out_specs=(
            P("dp", "rep"),
            P("dp", "rep"),
            P(("dp", "rep"), None),
            P("dp", None, "rep"),
            P("dp", "rep", None),
        ),
        check_vma=False,
    )
```

```python
import math

import jax
import jax.numpy as jnp
import numpy as np
from jax import lax
from jax.experimental import pallas as pl
from jax.experimental.pallas import tpu as pltpu
from jax.sharding import PartitionSpec as P

MESH = pl.DeviceIdType.MESH
D = 1664
NZ = 8
SLOTS = 9
BASE = 8
PLACES = 80
HROWS = 40
WIDE = 2 * D + 128
TWO = 2 * D
OUTW = 416
PRIO = 64
CAP = 1024
HID = 256
BF = jnp.bfloat16
F32 = jnp.float32
VMEM_LIMIT = 60 * 1024 * 1024
LAST = (((1,), (1,)), ((), ()))
FIRST = (((0,), (0,)), ((), ()))


def place():
    dp = lax.axis_index("dp")
    x = lax.axis_index("rep")
    z = dp // 16
    y = (dp // 2) % 8
    return dp, x, z, y // 2, y % 2, dp % 2


def compact_matrices():
    main = np.zeros((HROWS, 4 * BASE), np.float32)
    ninth = np.zeros((2, HROWS, 16), np.float32)
    for src in range(4):
        for slot in range(BASE):
            main[src * SLOTS + slot, src * BASE + slot] = 1.0
        for h in range(2):
            ninth[h, src * SLOTS + BASE, 4 * h + src] = 1.0
    return jnp.asarray(main, BF), jnp.asarray(ninth, BF)


def dot(a, b, dims=(((1,), (0,)), ((), ()))):
    return lax.dot_general(a, b, dims, preferred_element_type=F32)


def seat(r):
    return (r % 2) * 4 + r // 2


def remote(src, dst, ssem, rsem, device):
    return pltpu.make_async_remote_copy(
        src_ref=src, dst_ref=dst, send_sem=ssem, recv_sem=rsem, device_id=device, device_id_type=MESH
    )


def layer_kernel(
    ids_ref, prio_ref, gate_ref, tok_ref, cot_ref, win_ref, wout_ref, main_ref, ninth_ref,
    out_ref, dx_ref, gg_ref, gin_ref, gout_ref,
    sendbuf, sendx, landing, landx, rows, part, tot, cross, halves, full, ysum, yrecv, spread, spreadx, back, backx,
    ninths, result, chunk, gathered, gg, gg_in, seats, gcol, act_all, gpre_all, keep_all,
    send_a, recv_a, send_ax, recv_ax, send_b, recv_b, recv_h, send_c, recv_c, send_x, recv_x, send_hf, recv_hf,
    send_f, recv_f, send_y, recv_y, send_e, recv_e, send_ex, recv_ex, send_o, recv_o, send_g, recv_g,
):
    dp, x, z, pair, yp, c = place()
    own = (x + 16 - 2 * pair - z) % 4 == 0
    sibling, across = (dp + 1 - 2 * c, x), (dp + 2 - 4 * yp, x)
    xl, xr, xo = (x + 3) % 4, (x + 1) % 4, (x + 2) % 4
    right, left, far = (dp, xr), (dp, xl), (dp, xo)
    targets, sources = [], []
    for r in range(NZ):
        j = (z + r) % NZ
        targets.append(((j * 4 + (x + 16 - pair - j) % 4) * 4 + dp % 4, x))
        sources.append(((j * 4 + (x + 16 - pair - z) % 4) * 4 + dp % 4, x))

    barrier = pltpu.get_barrier_semaphore()

    def tell(device):
        pl.semaphore_signal(barrier, inc=1, device_id=device, device_id_type=MESH)

    near = (sibling, across, right, left, far)
    for device in near:
        tell(device)
    for r in range(1, NZ):
        tell(targets[r])
        if r != NZ // 2:
            tell(sources[r])

    @pl.when(jnp.logical_not(own))
    def _():
        tell(targets[0])

    lane = lax.broadcasted_iota(jnp.int32, (128, 128), 1)
    row = lax.broadcasted_iota(jnp.int32, (128, 128), 0)
    ids = [ids_ref[k : k + 1, :] for k in range(2)]
    hot = [(row == ids[k]).astype(F32) for k in range(2)]
    before = dot((hot[0] + hot[1]).astype(BF), (row < lane).astype(BF))
    tall = lax.broadcasted_iota(jnp.int32, (4 * PLACES, 128), 0)
    turned, gates_of, keys = [], [], []
    for k in range(2):
        slot = jnp.sum(hot[k] * before, axis=0, keepdims=True).astype(jnp.int32)
        ze = lax.shift_right_logical(ids[k], 2)
        pe = lax.bitwise_and(ids[k], 3)
        plane = lax.bitwise_and(pair + pe + ze + (4 - x), 3)
        distance = lax.bitwise_and(ze + (8 - z), 7)
        position = jnp.where(slot < BASE, distance * BASE + slot, NZ * BASE + distance) + plane * PLACES
        seat_of = (tall == position).astype(F32)
        seats[k] = seat_of.astype(BF)
        t = seat_of[0:PLACES]
        turned.append(t.astype(BF))
        gate = gate_ref[k : k + 1, :]
        gates_of.append(jnp.sum(t * gate, axis=1, keepdims=True))
        gcol[k] = jnp.broadcast_to(gate, (128, 128)).T
        key = (prio_ref[...] + (1 + PRIO * (1 - k))).astype(F32)
        keys.append(jnp.sum(t * key, axis=1, keepdims=True))
    cot16 = cot_ref[...]
    ninths[...] = jnp.zeros_like(ninths)
    for at, wide, value in (
        (0, D, dot(turned[0] + turned[1], tok_ref[...])),
        (D, D, gates_of[0] * dot(turned[0], cot16) + gates_of[1] * dot(turned[1], cot16)),
        (TWO, 128, jnp.broadcast_to(keys[0] + keys[1], (PLACES, 128))),
    ):
        value = value.astype(BF)
        sendbuf[:, :, at : at + wide] = value[0 : NZ * BASE].reshape(NZ, BASE, wide)
        single = value[NZ * BASE :].astype(F32)
        for r in range(NZ):
            sendx[r, :, at : at + wide] = single[r : r + 1]

    count = len(near) + 2 * (NZ - 1) - 1
    pl.semaphore_wait(barrier, jnp.where(own, count, count + 1))

    def out_copies(r):
        k = seat((NZ - r) % NZ)
        return (
            remote(sendbuf.at[r], landing.at[k], send_a.at[r], recv_a.at[k], targets[r]),
            remote(sendx.at[r], landx.at[k], send_ax.at[r], recv_ax.at[k], targets[r]),
        )

    def out_start(r):
        for copy in out_copies(r):
            copy.start()

    def in_wait(r):
        k = seat(r)
        remote(landing.at[k], landing.at[k], send_a.at[0], recv_a.at[k], sources[r]).wait_recv()
        remote(landx.at[k], landx.at[k], send_ax.at[0], recv_ax.at[k], sources[r]).wait_recv()

    def local(pairs):
        copies = [pltpu.make_async_copy(a, b, sem) for a, b, sem in pairs]
        for copy in copies:
            copy.start()
        for copy in copies:
            copy.wait()

    for r in (4, 2, 6):
        out_start(r)

    @pl.when(jnp.logical_not(own))
    def _():
        out_start(0)

    @pl.when(own)
    def _():
        local(
            (
                (sendbuf.at[0], landing.at[0], send_a.at[0]),
                (sendx.at[0], landx.at[0], send_ax.at[0]),
            )
        )

    @pl.when(jnp.logical_not(own))
    def _():
        in_wait(0)

    for r in (4, 2, 6):
        in_wait(r)
    for r in (3, 5, 1, 7):
        out_start(r)

    started = []

    def send(src, rsem, device):
        copy = remote(src, src, send_b.at[len(started)], rsem, device)
        copy.start()
        started.append(copy)

    def block(xx, yy):
        return (yy * 4 + xx) * 2 + c

    def whole(b, h, device):
        send(rows.at[b, h], recv_b.at[2 * b + h], device)

    def arrived(b, h):
        remote(rows.at[b, h], rows.at[b, h], send_b.at[0], recv_b.at[2 * b + h], sibling).wait_recv()

    mine = block(x, yp)
    other = block(x, 1 - yp)
    cut = (slice(0, 1792), slice(1792, WIDE))
    for h in range(2):
        if h:
            for r in (1, 3, 5, 7):
                in_wait(r)
        for i in range(4 * h, 4 * h + 4):
            ninths[i : i + 1, :] = landx[i]
        for lo in range(0, WIDE, 1152):
            got = landing[4 * h : 4 * h + 4, :, lo : lo + 1152].reshape(4 * BASE, 1152)
            extra = ninths[:, lo : lo + 1152].astype(BF)
            rows[mine, h, :, lo : lo + 1152] = (dot(main_ref[...], got) + dot(ninth_ref[h], extra)).astype(BF)
        for device in (across, right, left, sibling):
            whole(mine, h, device)
    for h in range(2):
        arrived(other, h)
        for device in (right, left, sibling):
            whole(other, h, device)

    win = win_ref[...]
    wout = wout_ref[...]

    def compute(yy, xx):
        u = yy * 4 + xx
        for h in range(2):
            arrived(2 * u + 1 - c, h)
        tok = rows[pl.ds(2 * u, 2), :, :, 0:D].reshape(4 * HROWS, D)
        grad = rows[pl.ds(2 * u, 2), :, :, D:TWO].reshape(4 * HROWS, D)
        pre = dot(tok, win)
        cdf = 0.5 * (1.0 + lax.erf(pre * (1.0 / math.sqrt(2.0))))
        density = jnp.exp(-0.5 * pre * pre) * (1.0 / math.sqrt(2.0 * math.pi))
        act = (pre * cdf).astype(BF)
        gpre = (dot(grad, wout, LAST) * (cdf + pre * density)).astype(BF)
        part[pl.ds(2 * u, 2), :, :, 0:D] = dot(act, wout).astype(BF).reshape(2, 2, HROWS, D)
        part[pl.ds(2 * u, 2), :, :, D:TWO] = dot(gpre, win, LAST).astype(BF).reshape(2, 2, HROWS, D)
        act_all[u] = act
        gpre_all[u] = gpre
        for h in range(2):
            core_copy(u, h).start()

    def core_copy(u, h):
        k = 2 * u + h
        return remote(part.at[2 * u + 1 - c, h], tot.at[u, h], send_c.at[k], recv_c.at[k], sibling)

    def merge(yy, xx, h):
        u = yy * 4 + xx
        core_copy(u, h).wait_recv()
        tot[u, h] = tot[u, h] + part[2 * u + c, h]

    def cross_copy(h):
        return remote(tot.at[(1 - yp) * 4 + xo, h], cross.at[h], send_x.at[h], recv_x.at[h], across)

    def half_copy(s, h):
        piece = tot.at[yp * 4 + xo, h, :, s * D : (s + 1) * D]
        k = 2 * s + h
        return remote(piece, halves.at[k], send_hf.at[k], recv_hf.at[k], right if s == 0 else left)

    def full_copy(o, s, h):
        u = (yp if o == 0 else 1 - yp) * 4 + (xr if s == 0 else xl)
        k = (2 * o + s) * 2 + h
        return remote(tot.at[u, h], full.at[k], send_f.at[k], recv_f.at[k], right if s == 0 else left)

    def y_copy(h):
        return remote(ysum.at[h], yrecv.at[h], send_y.at[h], recv_y.at[h], across)

    for h in range(2):
        b = block(xl, yp)
        arrived(b, h)
        send(rows.at[b, h, :, cut[0]], recv_h.at[2 * h], right)
        whole(b, h, sibling)
        b = block(xr, yp)
        arrived(b, h)
        send(rows.at[b, h, :, cut[1]], recv_h.at[2 * h + 1], left)
        whole(b, h, sibling)
    compute(yp, x)
    compute(1 - yp, x)
    for h in range(2):
        b = block(xo, yp)
        for s in range(2):
            piece = rows.at[b, h, :, cut[s]]
            remote(piece, piece, send_b.at[0], recv_h.at[2 * h + s], sibling).wait_recv()
        whole(b, h, across)
        whole(b, h, sibling)
    compute(yp, xl)
    compute(yp, xr)
    for h in range(2):
        for xx in (xl, xr):
            b = block(xx, 1 - yp)
            arrived(b, h)
            whole(b, h, sibling)
    compute(1 - yp, xr)
    compute(1 - yp, xl)
    for s in range(2):
        merge(1 - yp, xl if s else xr, 0)
        full_copy(1, s, 0).start()
    compute(yp, xo)
    for h in range(2):
        b = block(xo, 1 - yp)
        arrived(b, h)
        whole(b, h, sibling)
    compute(1 - yp, xo)

    merge(1 - yp, xo, 0)
    cross_copy(0).start()
    merge(1 - yp, xo, 1)
    for h in range(2):
        merge(yp, xo, h)
        merge(yp, xr, h)
        merge(yp, xl, h)
    merge(1 - yp, xr, 1)
    merge(1 - yp, xl, 1)
    for h in range(2):
        merge(1 - yp, x, h)
        merge(yp, x, h)

    level = lane[0:1, :].astype(F32)
    above = jnp.zeros((1, 128), F32)
    for u in range(8):
        key = rows[2 * u : 2 * u + 2, :, :, TWO:WIDE].reshape(4 * HROWS, 128).astype(F32)
        above = above + jnp.sum((key > level).astype(F32), axis=0, keepdims=True)
    cutoff = jnp.sum((above > CAP).astype(F32), axis=1, keepdims=True)
    for u in range(8):
        key = rows[2 * u : 2 * u + 2, :, :, TWO:WIDE].reshape(4 * HROWS, 128).astype(F32)
        keep_all[u] = (key > cutoff).astype(BF)
    keep_own = [(rows[mine, h, :, TWO : TWO + 1].astype(F32) > cutoff).astype(F32) for h in range(2)]

    for u in range(8):
        keep = jnp.concatenate([keep_all[u], keep_all[u]], axis=1)
        act_all[u] = act_all[u] * keep
        gpre_all[u] = gpre_all[u] * keep

    def cross_step(h):
        cross_copy(h).wait_recv()
        tot[yp * 4 + xo, h] = tot[yp * 4 + xo, h] + cross[h]
        half_copy(0, h).start()
        half_copy(1, h).start()

    def half_step(h):
        for s in range(2):
            half_copy(s, h).wait_recv()
            u = yp * 4 + (xr if s == 0 else xl)
            lanes = slice(s * D, (s + 1) * D)
            tot[u, h, :, lanes] = tot[u, h, :, lanes] + halves[2 * s + h]
            full_copy(0, s, h).start()

    def y_step(h):
        full_copy(1, 0, h).wait_recv()
        full_copy(1, 1, h).wait_recv()
        total = tot[(1 - yp) * 4 + x, h].astype(F32) + full[4 + h].astype(F32) + full[6 + h].astype(F32)
        ysum[h] = total.astype(BF)
        y_copy(h).start()

    cross_step(0)
    cross_copy(1).start()
    full_copy(1, 0, 1).start()
    full_copy(1, 1, 1).start()
    y_step(0)
    half_step(0)
    cross_step(1)
    y_step(1)
    half_step(1)

    def home_copies(r):
        k = (NZ - r) % NZ
        return (
            remote(spread.at[seat(r)], back.at[k], send_e.at[r], recv_e.at[k], sources[r]),
            remote(spreadx.at[seat(r)], backx.at[k], send_ex.at[r], recv_ex.at[k], sources[r]),
        )

    def home_start(r):
        for copy in home_copies(r):
            copy.start()

    def home_wait(r):
        remote(back.at[r], back.at[r], send_e.at[0], recv_e.at[r], targets[r]).wait_recv()
        remote(backx.at[r], backx.at[r], send_ex.at[0], recv_ex.at[r], targets[r]).wait_recv()

    for h in range(2):
        y_copy(h).wait_recv()
        total = tot[yp * 4 + x, h].astype(F32) + yrecv[h].astype(F32)
        for s in range(2):
            full_copy(0, s, h).wait_recv()
            total = total + full[2 * s + h].astype(F32)
        final = (total * keep_own[h]).astype(BF)
        for lo in (0, D):
            half = final[:, lo : lo + D]
            wide = dot(main_ref[...], half, FIRST).astype(BF)
            spread[4 * h : 4 * h + 4, :, lo : lo + D] = wide.reshape(4, BASE, D)
            single = dot(ninth_ref[h], half, FIRST)
            for i in range(4 * h, 4 * h + 4):
                spreadx[i, :, lo : lo + D] = single[i : i + 1]
        for r in (4 + h, 2 + h, 6 + h):
            home_start(r)
        if h:
            home_start(1)
        else:

            @pl.when(jnp.logical_not(own))
            def _():
                home_start(0)

            @pl.when(own)
            def _():
                local(
                    (
                        (spread.at[0], back.at[0], send_e.at[0]),
                        (spreadx.at[0], backx.at[0], send_ex.at[0]),
                    )
                )

    act_flat = act_all[...].reshape(32 * HROWS, HID)

    @pl.loop(0, 13)
    def _(i):
        at = pl.multiple_of(i * 128, 128)
        g = rows[:, :, :, pl.ds(D + at, 128)].reshape(32 * HROWS, 128)
        gout_ref[:, pl.ds(at, 128)] = dot(act_flat, g, FIRST).astype(BF)

    gpre_flat = gpre_all[...].reshape(32 * HROWS, HID)

    @pl.loop(0, 13)
    def _(i):
        at = pl.multiple_of(i * 128, 128)
        t = rows[:, :, :, pl.ds(at, 128)].reshape(32 * HROWS, 128)
        gin_ref[pl.ds(at, 128), :] = dot(t, gpre_flat, FIRST).astype(BF)

    for r in range(1, NZ):
        home_wait(r)

    @pl.when(jnp.logical_not(own))
    def _():
        home_wait(0)

    for r in range(NZ):
        ninths[r : r + 1, 0:TWO] = backx[r]
    result[0 : NZ * BASE, :] = back[...].reshape(NZ * BASE, TWO)
    result[NZ * BASE : PLACES, :] = ninths[:, 0:TWO].astype(BF)
    for k in range(2):
        value = result[:, k * D : (k + 1) * D]
        for i in range(4):
            chunk[i, k] = value[:, i * OUTW : (i + 1) * OUTW]

    def tail(src, dst, ssem, rsem):
        return [remote(src(n, to), dst(n), ssem.at[n - 1], rsem.at[n - 1], (dp, to)) for n, to in ((2, xo), (3, xr), (1, xl))]

    tails = tail(lambda n, to: chunk.at[to], lambda n: gathered.at[n], send_o, recv_o)
    for copy in tails:
        copy.start()
    cot = cot16.astype(F32)
    value = result[:, 0:D]
    gg0 = jnp.sum(cot * dot(seats[0, 0:PLACES], value, FIRST), axis=1, keepdims=True)
    gg1 = jnp.sum(cot * dot(seats[1, 0:PLACES], value, FIRST), axis=1, keepdims=True)
    gg[...] = jnp.where(lane == 0, gg0, jnp.where(lane == 1, gg1, 0.0)).reshape(4, 32, 128)
    last = tail(lambda n, to: gg.at[to], lambda n: gg_in.at[n - 1], send_g, recv_g)
    for copy in last:
        copy.start()
    gathered[0] = chunk[x]
    tails = tails + last
    for copy in tails:
        copy.wait_recv()
    gates = gg[x]
    for n in range(3):
        gates = gates + gg_in[n]
    gg_ref[...] = gates[:, 0:2]
    outs = gathered[:, 0].reshape(4 * PLACES, OUTW)
    mixed = gcol[0][:, 0:1] * dot(seats[0], outs, FIRST) + gcol[1][:, 0:1] * dot(seats[1], outs, FIRST)
    out_ref[...] = mixed.astype(BF)
    dx_ref[...] = dot(seats[0] + seats[1], gathered[:, 1].reshape(4 * PLACES, OUTW), FIRST).astype(BF)

    def sent(r):
        for copy in out_copies(r) + home_copies(r):
            copy.wait_send()

    for r in range(1, NZ):
        sent(r)

    @pl.when(jnp.logical_not(own))
    def _():
        sent(0)

    for copy in started + tails:
        copy.wait_send()
    for u in range(8):
        for h in range(2):
            core_copy(u, h).wait_send()
    for h in range(2):
        cross_copy(h).wait_send()
        y_copy(h).wait_send()
        for s in range(2):
            half_copy(s, h).wait_send()
            full_copy(0, s, h).wait_send()
            full_copy(1, s, h).wait_send()


def layer(*args):
    dma = pltpu.SemaphoreType.DMA
    vmem = pltpu.VMEM
    return pl.pallas_call(
        layer_kernel,
        out_shape=(
            jax.ShapeDtypeStruct((128, OUTW), BF),
            jax.ShapeDtypeStruct((128, OUTW), BF),
            jax.ShapeDtypeStruct((32, 2), F32),
            jax.ShapeDtypeStruct((D, HID), BF),
            jax.ShapeDtypeStruct((HID, D), BF),
        ),
        in_specs=[pl.BlockSpec(memory_space=vmem)] * 9,
        out_specs=[pl.BlockSpec(memory_space=vmem)] * 5,
        scratch_shapes=[
            vmem((NZ, BASE, WIDE), BF),
            vmem((NZ, 1, WIDE), F32),
            vmem((NZ, BASE, WIDE), BF),
            vmem((NZ, 1, WIDE), F32),
            vmem((16, 2, HROWS, WIDE), BF),
            vmem((16, 2, HROWS, TWO), BF),
            vmem((8, 2, HROWS, TWO), BF),
            vmem((2, HROWS, TWO), BF),
            vmem((4, HROWS, D), BF),
            vmem((8, HROWS, TWO), BF),
            vmem((2, HROWS, TWO), BF),
            vmem((2, HROWS, TWO), BF),
            vmem((NZ, BASE, TWO), BF),
            vmem((NZ, 1, TWO), F32),
            vmem((NZ, BASE, TWO), BF),
            vmem((NZ, 1, TWO), F32),
            vmem((16, WIDE), F32),
            vmem((PLACES, TWO), BF),
            vmem((4, 2, PLACES, OUTW), BF),
            vmem((4, 2, PLACES, OUTW), BF),
            vmem((4, 32, 128), F32),
            vmem((3, 32, 128), F32),
            vmem((2, 4 * PLACES, 128), BF),
            vmem((2, 128, 128), F32),
            vmem((8, 4 * HROWS, HID), BF),
            vmem((8, 4 * HROWS, HID), BF),
            vmem((8, 4 * HROWS, 128), BF),
            dma((8,)), dma((8,)), dma((8,)), dma((8,)), dma((32,)), dma((32,)), dma((4,)),
            dma((16,)), dma((16,)), dma((2,)), dma((2,)), dma((4,)), dma((4,)),
            dma((8,)), dma((8,)), dma((2,)), dma((2,)), dma((8,)), dma((8,)), dma((8,)), dma((8,)),
            dma((3,)), dma((3,)), dma((3,)), dma((3,)),
        ],
        compiler_params=pltpu.CompilerParams(collective_id=0, has_side_effects=True, vmem_limit_bytes=VMEM_LIMIT),
        name="layer",
    )(*args)


def body(tokens, expert_ids, priority, gate_values, weight_in, weight_out, cotangent):
    mixed, token_grad, gate_grad, grad_in, grad_out = layer(
        expert_ids.T, priority[None, :], gate_values.T, tokens, cotangent, weight_in[0], weight_out[0],
        *compact_matrices(),
    )
    return mixed, token_grad, gate_grad, grad_in[None], grad_out[None]


def solution(mesh):
    placed = (
        P("dp", None),
        P("dp", None),
        P("dp"),
        P("dp", None),
        P("dp", None, "rep"),
        P("dp", "rep", None),
        P("dp", None),
    )
    return jax.shard_map(
        body,
        mesh=mesh,
        in_specs=placed,
        out_specs=(
            P("dp", "rep"),
            P("dp", "rep"),
            P(("dp", "rep"), None),
            P("dp", None, "rep"),
            P("dp", "rep", None),
        ),
        check_vma=False,
    )
```

```python
import math

import jax
import jax.numpy as jnp
from jax import lax
from jax.experimental import pallas as pl
from jax.experimental.pallas import tpu as pltpu
from jax.sharding import PartitionSpec as P

MESH = pl.DeviceIdType.MESH
D = 1664
NZ = 8
SLOTS = 9
BASE = 8
PLACES = 80
HROWS = 40
PART = (40, 32)
WIDE = 2 * D + 128
TWO = 2 * D
OUTW = 416
PRIO = 64
CAP = 1024
HID = 256
BF = jnp.bfloat16
F32 = jnp.float32
VMEM_LIMIT = 60 * 1024 * 1024
LAST = (((1,), (1,)), ((), ()))
FIRST = (((0,), (0,)), ((), ()))


def place():
    dp = lax.axis_index("dp")
    x = lax.axis_index("rep")
    z = dp // 16
    y = (dp // 2) % 8
    return dp, x, z, y // 2, y % 2, dp % 2


def dot(a, b, dims=(((1,), (0,)), ((), ()))):
    return lax.dot_general(a, b, dims, preferred_element_type=F32)


def seat(r):
    return (r % 2) * 4 + r // 2


def remote(src, dst, ssem, rsem, device):
    return pltpu.make_async_remote_copy(
        src_ref=src, dst_ref=dst, send_sem=ssem, recv_sem=rsem, device_id=device, device_id_type=MESH
    )


def layer_kernel(
    ids_ref, prio_ref, gate_ref, tok_ref, cot_ref, win_ref, wout_ref,
    out_ref, dx_ref, gg_ref, gin_ref, gout_ref,
    sendbuf, sendx, landing, landx, rows, part, tot, cross, halves, full, ysum, yrecv, spread, spreadx, back, backx,
    ninths, result, chunk, gathered, gg, gg_in, seats,
    win_in, wout_in, gin, gout, act_all, gpre_all, keep_all,
    send_a, recv_a, send_ax, recv_ax, send_b, recv_b, recv_h, send_c, recv_c, send_x, recv_x, send_hf, recv_hf,
    send_f, recv_f, send_y, recv_y, send_e, recv_e, send_ex, recv_ex, send_o, recv_o, send_g, recv_g, local_sem,
):
    dp, x, z, pair, yp, c = place()
    own = (x + 16 - 2 * pair - z) % 4 == 0
    sibling, across = (dp + 1 - 2 * c, x), (dp + 2 - 4 * yp, x)
    xl, xr, xo = (x + 3) % 4, (x + 1) % 4, (x + 2) % 4
    right, left, far = (dp, xr), (dp, xl), (dp, xo)
    targets, sources = [], []
    for r in range(NZ):
        j = (z + r) % NZ
        targets.append(((j * 4 + (x + 16 - pair - j) % 4) * 4 + dp % 4, x))
        sources.append(((j * 4 + (x + 16 - pair - z) % 4) * 4 + dp % 4, x))

    weights_in = pltpu.make_async_copy(win_ref, win_in, local_sem.at[0])
    weights_out = pltpu.make_async_copy(wout_ref, wout_in, local_sem.at[1])
    weights_in.start()
    weights_out.start()

    barrier = pltpu.get_barrier_semaphore()

    def tell(device):
        pl.semaphore_signal(barrier, inc=1, device_id=device, device_id_type=MESH)

    near = (sibling, across, right, left, far)
    for device in near:
        tell(device)
    for r in range(1, NZ):
        tell(targets[r])
        if r != NZ // 2:
            tell(sources[r])

    @pl.when(jnp.logical_not(own))
    def _():
        tell(targets[0])

    lane = lax.broadcasted_iota(jnp.int32, (128, 128), 1)
    row = lax.broadcasted_iota(jnp.int32, (128, 128), 0)
    ids = [ids_ref[k : k + 1, :] for k in range(2)]
    hot = [(row == ids[k]).astype(F32) for k in range(2)]
    before = dot((hot[0] + hot[1]).astype(BF), (row < lane).astype(BF))
    tall = lax.broadcasted_iota(jnp.int32, (4 * PLACES, 128), 0)
    turned, gates_of, keys = [], [], []
    for k in range(2):
        slot = jnp.sum(hot[k] * before, axis=0, keepdims=True).astype(jnp.int32)
        ze = lax.shift_right_logical(ids[k], 2)
        pe = lax.bitwise_and(ids[k], 3)
        plane = lax.bitwise_and(pair + pe + ze + (4 - x), 3)
        distance = lax.bitwise_and(ze + (8 - z), 7)
        spot = lax.bitwise_and(distance, 1) * 4 + lax.shift_right_logical(distance, 1)
        late = lax.shift_left(lax.shift_right_logical(spot, 2), 4)
        position = jnp.where(slot < BASE, spot * BASE + slot + late, 4 * BASE + spot) + plane * PLACES
        seat_of = (tall == position).astype(F32)
        seats[k] = seat_of.astype(BF)
        t = seat_of[0:PLACES]
        turned.append(t.astype(BF))
        gate = gate_ref[k : k + 1, :]
        gates_of.append(jnp.sum(t * gate, axis=1, keepdims=True))
        key = (prio_ref[...] + (1 + PRIO * (1 - k))).astype(F32)
        keys.append(jnp.sum(t * key, axis=1, keepdims=True))
    cot16 = cot_ref[...]
    ninths[...] = jnp.zeros_like(ninths)
    rows[:, 1, PART[1] :, :] = jnp.zeros((16, HROWS - PART[1], WIDE), BF)
    for at, wide, value in (
        (0, D, dot(turned[0] + turned[1], tok_ref[...])),
        (D, D, gates_of[0] * dot(turned[0], cot16) + gates_of[1] * dot(turned[1], cot16)),
        (TWO, 128, jnp.broadcast_to(keys[0] + keys[1], (PLACES, 128))),
    ):
        value = value.astype(BF)
        sendbuf[0:4, :, at : at + wide] = value[0:32].reshape(4, BASE, wide)
        sendbuf[4:8, :, at : at + wide] = value[48:80].reshape(4, BASE, wide)
        single = value[32:48].astype(F32)
        for r in range(NZ):
            sendx[r, :, at : at + wide] = single[r : r + 1]

    count = len(near) + 2 * (NZ - 1) - 1
    pl.semaphore_wait(barrier, jnp.where(own, count, count + 1))

    def out_main(r):
        k = seat((NZ - r) % NZ)
        return remote(sendbuf.at[seat(r)], landing.at[k], send_a.at[r], recv_a.at[k], targets[r])

    def out_ninth(r):
        k = seat((NZ - r) % NZ)
        return remote(sendx.at[seat(r)], landx.at[k], send_ax.at[r], recv_ax.at[k], targets[r])

    def in_main(r):
        k = seat(r)
        return remote(landing.at[k], landing.at[k], send_a.at[0], recv_a.at[k], sources[r])

    def in_ninth(r):
        k = seat(r)
        return remote(landx.at[k], landx.at[k], send_ax.at[0], recv_ax.at[k], sources[r])

    def local(pairs):
        copies = [pltpu.make_async_copy(a, b, sem) for a, b, sem in pairs]
        for copy in copies:
            copy.start()
        for copy in copies:
            copy.wait()

    for r in (4, 2, 6):
        out_main(r).start()

    @pl.when(jnp.logical_not(own))
    def _():
        out_main(0).start()
        out_ninth(0).start()

    for r in (4, 3, 5, 2, 6, 1, 7):
        out_ninth(r).start()

    @pl.when(own)
    def _():
        local(
            (
                (sendbuf.at[0], landing.at[0], send_a.at[0]),
                (sendx.at[0], landx.at[0], send_ax.at[0]),
            )
        )

    @pl.when(jnp.logical_not(own))
    def _():
        in_main(0).wait_recv()
        in_ninth(0).wait_recv()

    for r in (4, 2, 6):
        in_main(r).wait_recv()
    for r in range(1, NZ):
        in_ninth(r).wait_recv()
    for r in (3, 5, 1, 7):
        out_main(r).start()

    started = []

    def send(src, rsem, device):
        copy = remote(src, src, send_b.at[len(started)], rsem, device)
        copy.start()
        started.append(copy)

    def block(xx, yy):
        return (yy * 4 + xx) * 2 + c

    def whole(b, h, device):
        send(rows.at[b, h, 0 : PART[h]], recv_b.at[2 * b + h], device)

    def arrived(b, h):
        remote(rows.at[b, h, 0 : PART[h]], rows.at[b, h, 0 : PART[h]], send_b.at[0], recv_b.at[2 * b + h], sibling).wait_recv()

    mine = block(x, yp)
    other = block(x, 1 - yp)
    cut = (slice(0, 1792), slice(1792, WIDE))

    def compute(yy, xx, hs=(0, 1)):
        u = yy * 4 + xx
        n = len(hs)
        at = slice(hs[0], hs[-1] + 1)
        for h in hs:
            arrived(2 * u + 1 - c, h)
        tok = rows[pl.ds(2 * u, 2), at, :, 0:D].reshape(2 * n * HROWS, D)
        grad = rows[pl.ds(2 * u, 2), at, :, D:TWO].reshape(2 * n * HROWS, D)
        pre = dot(tok, win_in[...])
        cdf = 0.5 * (1.0 + lax.erf(pre * (1.0 / math.sqrt(2.0))))
        density = jnp.exp(-0.5 * pre * pre) * (1.0 / math.sqrt(2.0 * math.pi))
        act = (pre * cdf).astype(BF)
        gpre = (dot(grad, wout_in[...], LAST) * (cdf + pre * density)).astype(BF)
        part[pl.ds(2 * u, 2), at, :, 0:D] = dot(act, wout_in[...]).astype(BF).reshape(2, n, HROWS, D)
        part[pl.ds(2 * u, 2), at, :, D:TWO] = dot(gpre, win_in[...], LAST).astype(BF).reshape(2, n, HROWS, D)
        act_all[u, :, at] = act.reshape(2, n, HROWS, HID)
        gpre_all[u, :, at] = gpre.reshape(2, n, HROWS, HID)
        for h in hs:
            core_copy(u, h).start()

    def core_copy(u, h):
        k = 2 * u + h
        return remote(part.at[2 * u + 1 - c, h, 0 : PART[h]], tot.at[u, h, 0 : PART[h]], send_c.at[k], recv_c.at[k], sibling)

    def merge(yy, xx, h):
        u = yy * 4 + xx
        core_copy(u, h).wait_recv()
        n = PART[h]
        tot[u, h, 0:n] = tot[u, h, 0:n] + part[2 * u + c, h, 0:n]

    def cross_copy(h):
        return remote(tot.at[(1 - yp) * 4 + xo, h, 0 : PART[h]], cross.at[h, 0 : PART[h]], send_x.at[h], recv_x.at[h], across)

    def half_copy(s, h):
        piece = tot.at[yp * 4 + xo, h, 0 : PART[h], s * D : (s + 1) * D]
        k = 2 * s + h
        return remote(piece, halves.at[k, 0 : PART[h]], send_hf.at[k], recv_hf.at[k], right if s == 0 else left)

    def full_copy(o, s, h):
        u = (yp if o == 0 else 1 - yp) * 4 + (xr if s == 0 else xl)
        k = (2 * o + s) * 2 + h
        return remote(tot.at[u, h, 0 : PART[h]], full.at[k, 0 : PART[h]], send_f.at[k], recv_f.at[k], right if s == 0 else left)

    def y_copy(h):
        return remote(ysum.at[h, 0 : PART[h]], yrecv.at[h, 0 : PART[h]], send_y.at[h], recv_y.at[h], across)

    def own_rows(h):
        rows[mine, h, 0:32, :] = landing[4 * h : 4 * h + 4].reshape(4 * BASE, WIDE)
        if h == 0:
            for i in range(NZ):
                ninths[i : i + 1, :] = landx[i]
            rows[mine, h, 32:40, :] = ninths[0:NZ, :].astype(BF)
        for device in (across, right, left, sibling):
            whole(mine, h, device)

    def from_row(h):
        b = block(xl, yp)
        arrived(b, h)
        send(rows.at[b, h, 0 : PART[h], cut[0]], recv_h.at[2 * h], right)
        whole(b, h, sibling)
        b = block(xr, yp)
        arrived(b, h)
        send(rows.at[b, h, 0 : PART[h], cut[1]], recv_h.at[2 * h + 1], left)
        whole(b, h, sibling)

    def from_across(h):
        arrived(other, h)
        for device in (right, left, sibling):
            whole(other, h, device)

    def from_far(h):
        b = block(xo, yp)
        for s in range(2):
            piece = rows.at[b, h, 0 : PART[h], cut[s]]
            remote(piece, piece, send_b.at[0], recv_h.at[2 * h + s], sibling).wait_recv()
        whole(b, h, across)
        whole(b, h, sibling)

    def from_other_row(xx, h):
        b = block(xx, 1 - yp)
        arrived(b, h)
        whole(b, h, sibling)

    own_rows(0)
    from_row(0)
    from_across(0)
    for r in (1, 3, 5, 7):
        in_main(r).wait_recv()
    own_rows(1)
    weights_in.wait()
    weights_out.wait()
    from_far(0)
    for yy, xx in ((yp, x), (1 - yp, x), (yp, xl), (yp, xr)):
        compute(yy, xx, (0,))
    from_row(1)
    from_across(1)
    compute(yp, xo, (0,))
    compute(yp, x, (1,))
    compute(1 - yp, x, (1,))
    from_far(1)
    compute(yp, xl, (1,))
    compute(yp, xr, (1,))
    for h in range(2):
        from_other_row(xl, h)
        from_other_row(xr, h)
    compute(1 - yp, xr)
    compute(1 - yp, xl)
    from_other_row(xo, 0)
    compute(1 - yp, xo, (0,))
    for h in range(2):
        for s in range(2):
            merge(1 - yp, xl if s else xr, h)
            full_copy(1, s, h).start()
    compute(yp, xo, (1,))
    merge(1 - yp, xo, 0)
    cross_copy(0).start()
    from_other_row(xo, 1)
    compute(1 - yp, xo, (1,))
    for h in range(2):
        merge(yp, xo, h)
    merge(1 - yp, xo, 1)
    cross_copy(1).start()
    for h in range(2):
        merge(yp, xr, h)
        merge(yp, xl, h)
    for h in range(2):
        merge(1 - yp, x, h)
        merge(yp, x, h)

    level = lane[0:1, :].astype(F32)
    above = jnp.zeros((1, 128), F32)
    for u in range(8):
        key = rows[2 * u : 2 * u + 2, :, :, TWO:WIDE].reshape(4 * HROWS, 128).astype(F32)
        above = above + jnp.sum((key > level).astype(F32), axis=0, keepdims=True)
    cutoff = jnp.sum((above > CAP).astype(F32), axis=1, keepdims=True)
    for u in range(8):
        key = rows[2 * u : 2 * u + 2, :, :, TWO:WIDE].reshape(4 * HROWS, 128).astype(F32)
        keep_all[u] = (key > cutoff).astype(BF)
    keep_own = [(rows[mine, h, 0 : PART[h], TWO : TWO + 1].astype(F32) > cutoff).astype(F32) for h in range(2)]

    for u in range(8):
        keep = jnp.concatenate([keep_all[u], keep_all[u]], axis=1).reshape(2, 2, HROWS, HID)
        act_all[u] = act_all[u] * keep
        gpre_all[u] = gpre_all[u] * keep

    def out_gradients(lo, hi):
        @pl.loop(lo, hi)
        def _(i):
            at = pl.multiple_of(i * 128, 128)
            g = rows[:, :, :, pl.ds(D + at, 128)].reshape(32 * HROWS, 128)
            gout[:, pl.ds(at, 128)] = dot(act_all[...].reshape(32 * HROWS, HID), g, FIRST).astype(BF)

    def in_gradients(lo, hi):
        @pl.loop(lo, hi)
        def _(i):
            at = pl.multiple_of(i * 128, 128)
            t = rows[:, :, :, pl.ds(at, 128)].reshape(32 * HROWS, 128)
            gin[pl.ds(at, 128), :] = dot(t, gpre_all[...].reshape(32 * HROWS, HID), FIRST).astype(BF)

    def cross_step(h):
        cross_copy(h).wait_recv()
        n = PART[h]
        tot[yp * 4 + xo, h, 0:n] = tot[yp * 4 + xo, h, 0:n] + cross[h, 0:n]
        half_copy(0, h).start()
        half_copy(1, h).start()

    def half_step(h):
        for s in range(2):
            half_copy(s, h).wait_recv()
            u = yp * 4 + (xr if s == 0 else xl)
            lanes = slice(s * D, (s + 1) * D)
            n = PART[h]
            tot[u, h, 0:n, lanes] = tot[u, h, 0:n, lanes] + halves[2 * s + h, 0:n]
            full_copy(0, s, h).start()

    def y_step(h):
        full_copy(1, 0, h).wait_recv()
        full_copy(1, 1, h).wait_recv()
        n = PART[h]
        total = tot[(1 - yp) * 4 + x, h, 0:n].astype(F32) + full[4 + h, 0:n].astype(F32) + full[6 + h, 0:n].astype(F32)
        ysum[h, 0:n] = total.astype(BF)
        y_copy(h).start()

    cross_step(0)
    y_step(0)
    half_step(0)
    cross_step(1)
    y_step(1)
    out_gradients(0, 5)
    half_step(1)
    out_gradients(5, 10)

    def home_main(r):
        k = seat((NZ - r) % NZ)
        return remote(spread.at[seat(r)], back.at[k], send_e.at[r], recv_e.at[k], sources[r])

    def home_ninth(r):
        k = seat((NZ - r) % NZ)
        return remote(spreadx.at[seat(r)], backx.at[k], send_ex.at[r], recv_ex.at[k], sources[r])

    def home_wait(r):
        k = seat(r)
        remote(back.at[k], back.at[k], send_e.at[0], recv_e.at[k], targets[r]).wait_recv()

    def ninth_wait(r):
        k = seat(r)
        remote(backx.at[k], backx.at[k], send_ex.at[0], recv_ex.at[k], targets[r]).wait_recv()

    for h in range(2):
        y_copy(h).wait_recv()
        n = PART[h]
        total = tot[yp * 4 + x, h, 0:n].astype(F32) + yrecv[h, 0:n].astype(F32)
        for s in range(2):
            full_copy(0, s, h).wait_recv()
            total = total + full[2 * s + h, 0:n].astype(F32)
        final = (total * keep_own[h]).astype(BF)
        spread[4 * h : 4 * h + 4] = final[0:32].reshape(4, BASE, TWO)
        if h == 0:
            single = final[32:40].astype(F32)
            for i in range(NZ):
                spreadx[i] = single[i : i + 1]
        for r in (4 + h, 2 + h, 6 + h):
            home_main(r).start()
        if h:
            home_main(1).start()
        else:

            @pl.when(jnp.logical_not(own))
            def _():
                home_main(0).start()
                home_ninth(0).start()

            for r in (4, 3, 5, 2, 6, 1, 7):
                home_ninth(r).start()

            @pl.when(own)
            def _():
                local(
                    (
                        (spread.at[0], back.at[0], send_e.at[0]),
                        (spreadx.at[0], backx.at[0], send_ex.at[0]),
                    )
                )

    out_gradients(10, 13)
    gradients_out = pltpu.make_async_copy(gout, gout_ref, local_sem.at[2])
    gradients_out.start()
    in_gradients(0, 4)

    def tail(src, dst, ssem, rsem):
        return [remote(src(n, to), dst(n), ssem.at[n - 1], rsem.at[n - 1], (dp, to)) for n, to in ((2, xo), (3, xr), (1, xl))]

    tails = []
    parts = (slice(0, 48), slice(48, PLACES))

    def result_part(p):
        for k in range(2):
            value = result[parts[p], k * D : (k + 1) * D]
            for i in range(4):
                chunk[i, k, parts[p], :] = value[:, i * OUTW : (i + 1) * OUTW]
        copies = tail(
            lambda n, to: chunk.at[to, :, parts[p]], lambda n: gathered.at[n, :, parts[p]], send_o.at[p], recv_o.at[p]
        )
        for copy in copies:
            copy.start()
        tails.extend(copies)

    for r in (4, 2, 6):
        home_wait(r)

    @pl.when(jnp.logical_not(own))
    def _():
        home_wait(0)
        ninth_wait(0)

    for r in range(1, NZ):
        ninth_wait(r)
    for r in range(NZ):
        ninths[r : r + 1, 0:TWO] = backx[r]
    result[0:32, :] = back[0:4].reshape(4 * BASE, TWO)
    result[32:48, :] = ninths[:, 0:TWO].astype(BF)
    result_part(0)
    in_gradients(4, 13)
    gradients_in = pltpu.make_async_copy(gin, gin_ref, local_sem.at[3])
    gradients_in.start()
    for r in (1, 3, 5, 7):
        home_wait(r)
    result[48:PLACES, :] = back[4:8].reshape(4 * BASE, TWO)
    result_part(1)
    cot = cot16.astype(F32)
    value = result[:, 0:D]
    gg0 = jnp.sum(cot * dot(seats[0, 0:PLACES], value, FIRST), axis=1, keepdims=True)
    gg1 = jnp.sum(cot * dot(seats[1, 0:PLACES], value, FIRST), axis=1, keepdims=True)
    gg[...] = jnp.where(lane == 0, gg0, jnp.where(lane == 1, gg1, 0.0)).reshape(4, 32, 128)
    last = tail(lambda n, to: gg.at[to], lambda n: gg_in.at[n - 1], send_g, recv_g)
    for copy in last:
        copy.start()
    gathered[0] = chunk[x]
    tails.extend(last)
    for copy in tails:
        copy.wait_recv()
    gates = gg[x]
    for n in range(3):
        gates = gates + gg_in[n]
    gg_ref[...] = gates[:, 0:2]
    outs = gathered[:, 0].reshape(4 * PLACES, OUTW)
    mixed = gate_ref[0:1, :] * dot(outs, seats[0], FIRST) + gate_ref[1:2, :] * dot(outs, seats[1], FIRST)
    out_ref[...] = mixed.astype(BF)
    moved = gathered[:, 1].reshape(4 * PLACES, OUTW)
    dx_ref[...] = dot(moved, seats[0] + seats[1], FIRST).astype(BF)

    gradients_out.wait()
    gradients_in.wait()

    def sent(r):
        for copy in (out_main(r), out_ninth(r), home_main(r), home_ninth(r)):
            copy.wait_send()

    for r in range(1, NZ):
        sent(r)

    @pl.when(jnp.logical_not(own))
    def _():
        sent(0)

    for copy in started + tails:
        copy.wait_send()
    for u in range(8):
        for h in range(2):
            core_copy(u, h).wait_send()
    for h in range(2):
        cross_copy(h).wait_send()
        y_copy(h).wait_send()
        for s in range(2):
            half_copy(s, h).wait_send()
            full_copy(0, s, h).wait_send()
            full_copy(1, s, h).wait_send()


def layer(*args):
    dma = pltpu.SemaphoreType.DMA
    vmem = pltpu.VMEM
    return pl.pallas_call(
        layer_kernel,
        out_shape=(
            jax.ShapeDtypeStruct((OUTW, 128), BF),
            jax.ShapeDtypeStruct((OUTW, 128), BF),
            jax.ShapeDtypeStruct((32, 2), F32),
            jax.ShapeDtypeStruct((D, HID), BF),
            jax.ShapeDtypeStruct((HID, D), BF),
        ),
        in_specs=[pl.BlockSpec(memory_space=vmem)] * 5
        + [pl.BlockSpec(memory_space=pl.ANY)] * 2,
        out_specs=[pl.BlockSpec(memory_space=vmem)] * 3 + [pl.BlockSpec(memory_space=pl.ANY)] * 2,
        scratch_shapes=[
            vmem((NZ, BASE, WIDE), BF),
            vmem((NZ, 1, WIDE), F32),
            vmem((NZ, BASE, WIDE), BF),
            vmem((NZ, 1, WIDE), F32),
            vmem((16, 2, HROWS, WIDE), BF),
            vmem((16, 2, HROWS, TWO), BF),
            vmem((8, 2, HROWS, TWO), BF),
            vmem((2, HROWS, TWO), BF),
            vmem((4, HROWS, D), BF),
            vmem((8, HROWS, TWO), BF),
            vmem((2, HROWS, TWO), BF),
            vmem((2, HROWS, TWO), BF),
            vmem((NZ, BASE, TWO), BF),
            vmem((NZ, 1, TWO), F32),
            vmem((NZ, BASE, TWO), BF),
            vmem((NZ, 1, TWO), F32),
            vmem((16, WIDE), F32),
            vmem((PLACES, TWO), BF),
            vmem((4, 2, PLACES, OUTW), BF),
            vmem((4, 2, PLACES, OUTW), BF),
            vmem((4, 32, 128), F32),
            vmem((3, 32, 128), F32),
            vmem((2, 4 * PLACES, 128), BF),
            vmem((D, HID), BF),
            vmem((HID, D), BF),
            vmem((D, HID), BF),
            vmem((HID, D), BF),
            vmem((8, 2, 2, HROWS, HID), BF),
            vmem((8, 2, 2, HROWS, HID), BF),
            vmem((8, 4 * HROWS, 128), BF),
            dma((8,)), dma((8,)), dma((8,)), dma((8,)), dma((32,)), dma((32,)), dma((4,)),
            dma((16,)), dma((16,)), dma((2,)), dma((2,)), dma((4,)), dma((4,)),
            dma((8,)), dma((8,)), dma((2,)), dma((2,)), dma((8,)), dma((8,)), dma((8,)), dma((8,)),
            dma((2, 3)), dma((2, 3)), dma((3,)), dma((3,)), dma((4,)),
        ],
        compiler_params=pltpu.CompilerParams(collective_id=0, has_side_effects=True, vmem_limit_bytes=VMEM_LIMIT),
        name="layer",
    )(*args)


def body(tokens, expert_ids, priority, gate_values, weight_in, weight_out, cotangent):
    mixed, token_grad, gate_grad, grad_in, grad_out = layer(
        expert_ids.T, priority[None, :], gate_values.T, tokens, cotangent, weight_in[0], weight_out[0],
    )
    return mixed.T, token_grad.T, gate_grad, grad_in[None], grad_out[None]


def solution(mesh):
    placed = (
        P("dp", None),
        P("dp", None),
        P("dp"),
        P("dp", None),
        P("dp", None, "rep"),
        P("dp", "rep", None),
        P("dp", None),
    )
    return jax.shard_map(
        body,
        mesh=mesh,
        in_specs=placed,
        out_specs=(
            P("dp", "rep"),
            P("dp", "rep"),
            P(("dp", "rep"), None),
            P("dp", None, "rep"),
            P("dp", "rep", None),
        ),
        check_vma=False,
    )
```

```python
import math

import jax
import jax.numpy as jnp
from jax import lax
from jax.experimental import pallas as pl
from jax.experimental.pallas import tpu as pltpu
from jax.sharding import PartitionSpec as P

MESH = pl.DeviceIdType.MESH
D = 1664
NZ = 8
SLOTS = 9
BASE = 8
PLACES = 80
HROWS = 40
PART = (40, 32)
WIDE = 2 * D + 128
TWO = 2 * D
PAIR = D + 128
OUTW = 416
PRIO = 64
CAP = 1024
HID = 256
BF = jnp.bfloat16
F32 = jnp.float32
VMEM_LIMIT = 60 * 1024 * 1024
LAST = (((1,), (1,)), ((), ()))
FIRST = (((0,), (0,)), ((), ()))


def place():
    dp = lax.axis_index("dp")
    x = lax.axis_index("rep")
    z = dp // 16
    y = (dp // 2) % 8
    return dp, x, z, y // 2, y % 2, dp % 2


def dot(a, b, dims=(((1,), (0,)), ((), ()))):
    return lax.dot_general(a, b, dims, preferred_element_type=F32)


def seat(r):
    return (r % 2) * 4 + r // 2


def remote(src, dst, ssem, rsem, device):
    return pltpu.make_async_remote_copy(
        src_ref=src, dst_ref=dst, send_sem=ssem, recv_sem=rsem, device_id=device, device_id_type=MESH
    )


def layer_kernel(
    ids_ref, prio_ref, gate_ref, tok_ref, cot_ref, win_ref, wout_ref,
    out_ref, dx_ref, gg_ref, gin_ref, gout_ref,
    sendbuf, sendx, landing, landx, rows, part, tot, cross, halves, full, ysum, yrecv, spread, spreadx, back, backx,
    ninths, result, chunk, gathered, gg, gg_in, seats,
    win_in, wout_in, gin, gout, act_all, gpre_all, keep_all,
    send_a, recv_a, send_ax, recv_ax, send_b, recv_b, recv_h, send_c, recv_c, send_x, recv_x, send_hf, recv_hf,
    send_f, recv_f, send_y, recv_y, send_e, recv_e, send_ex, recv_ex, send_o, recv_o, send_g, recv_g, local_sem,
):
    dp, x, z, pair, yp, c = place()
    own = (x + 16 - 2 * pair - z) % 4 == 0
    sibling, across = (dp + 1 - 2 * c, x), (dp + 2 - 4 * yp, x)
    xl, xr, xo = (x + 3) % 4, (x + 1) % 4, (x + 2) % 4
    right, left, far = (dp, xr), (dp, xl), (dp, xo)
    targets, sources = [], []
    for r in range(NZ):
        j = (z + r) % NZ
        targets.append(((j * 4 + (x + 16 - pair - j) % 4) * 4 + dp % 4, x))
        sources.append(((j * 4 + (x + 16 - pair - z) % 4) * 4 + dp % 4, x))

    weights_in = pltpu.make_async_copy(win_ref, win_in, local_sem.at[0])
    weights_out = pltpu.make_async_copy(wout_ref, wout_in, local_sem.at[1])
    weights_in.start()
    weights_out.start()

    barrier = pltpu.get_barrier_semaphore()

    def tell(device):
        pl.semaphore_signal(barrier, inc=1, device_id=device, device_id_type=MESH)

    near = (sibling, across, right, left, far)
    for device in near:
        tell(device)
    for r in range(1, NZ):
        tell(targets[r])
        if r != NZ // 2:
            tell(sources[r])

    @pl.when(jnp.logical_not(own))
    def _():
        tell(targets[0])

    lane = lax.broadcasted_iota(jnp.int32, (128, 128), 1)
    row = lax.broadcasted_iota(jnp.int32, (128, 128), 0)
    ids = [ids_ref[k : k + 1, :] for k in range(2)]
    hot = [(row == ids[k]).astype(F32) for k in range(2)]
    before = dot((hot[0] + hot[1]).astype(BF), (row < lane).astype(BF))
    tall = lax.broadcasted_iota(jnp.int32, (4 * PLACES, 128), 0)
    turned, gates_of, keys = [], [], []
    for k in range(2):
        slot = jnp.sum(hot[k] * before, axis=0, keepdims=True).astype(jnp.int32)
        ze = lax.shift_right_logical(ids[k], 2)
        pe = lax.bitwise_and(ids[k], 3)
        plane = lax.bitwise_and(pair + pe + ze + (4 - x), 3)
        distance = lax.bitwise_and(ze + (8 - z), 7)
        spot = lax.bitwise_and(distance, 1) * 4 + lax.shift_right_logical(distance, 1)
        late = lax.shift_left(lax.shift_right_logical(spot, 2), 4)
        position = jnp.where(slot < BASE, spot * BASE + slot + late, 4 * BASE + spot) + plane * PLACES
        seat_of = (tall == position).astype(F32)
        seats[k] = seat_of.astype(BF)
        t = seat_of[0:PLACES]
        turned.append(t.astype(BF))
        gate = gate_ref[k : k + 1, :]
        gates_of.append(jnp.sum(t * gate, axis=1, keepdims=True))
        key = (prio_ref[...] + (1 + PRIO * (1 - k))).astype(F32)
        keys.append(jnp.sum(t * key, axis=1, keepdims=True))
    cot16 = cot_ref[...]
    singles = []
    ninths[...] = jnp.zeros_like(ninths)
    rows[:, 1, PART[1] :, :] = jnp.zeros((16, HROWS - PART[1], WIDE), BF)
    for at, wide, value in (
        (0, D, dot(turned[0] + turned[1], tok_ref[...])),
        (D, D, gates_of[0] * dot(turned[0], cot16) + gates_of[1] * dot(turned[1], cot16)),
        (TWO, 128, jnp.broadcast_to(keys[0] + keys[1], (PLACES, 128))),
    ):
        value = value.astype(BF)
        sendbuf[0:4, :, at : at + wide] = value[0:32].reshape(4, BASE, wide)
        sendbuf[4:8, :, at : at + wide] = value[48:80].reshape(4, BASE, wide)
        singles.append(value[32:48].astype(F32))
    top = jnp.concatenate([singles[0], singles[2]], axis=1)
    bottom = jnp.concatenate([singles[1], jnp.zeros((16, 128), F32)], axis=1)
    for r in range(NZ):
        sendx[r] = jnp.concatenate([top[r : r + 1], bottom[r : r + 1]], axis=0).astype(BF)

    count = len(near) + 2 * (NZ - 1) - 1
    pl.semaphore_wait(barrier, jnp.where(own, count, count + 1))

    def out_main(r):
        k = seat((NZ - r) % NZ)
        return remote(sendbuf.at[seat(r)], landing.at[k], send_a.at[r], recv_a.at[k], targets[r])

    def out_ninth(r):
        k = seat((NZ - r) % NZ)
        return remote(sendx.at[seat(r)], landx.at[k], send_ax.at[r], recv_ax.at[k], targets[r])

    def in_main(r):
        k = seat(r)
        return remote(landing.at[k], landing.at[k], send_a.at[0], recv_a.at[k], sources[r])

    def in_ninth(r):
        k = seat(r)
        return remote(landx.at[k], landx.at[k], send_ax.at[0], recv_ax.at[k], sources[r])

    def local(pairs):
        copies = [pltpu.make_async_copy(a, b, sem) for a, b, sem in pairs]
        for copy in copies:
            copy.start()
        for copy in copies:
            copy.wait()

    for r in (4, 2, 6):
        out_main(r).start()

    @pl.when(jnp.logical_not(own))
    def _():
        out_main(0).start()
        out_ninth(0).start()

    for r in (4, 3, 5, 2, 6, 1, 7):
        out_ninth(r).start()

    @pl.when(own)
    def _():
        local(
            (
                (sendbuf.at[0], landing.at[0], send_a.at[0]),
                (sendx.at[0], landx.at[0], send_ax.at[0]),
            )
        )

    @pl.when(jnp.logical_not(own))
    def _():
        in_main(0).wait_recv()
        in_ninth(0).wait_recv()

    for r in (4, 2, 6):
        in_main(r).wait_recv()
    for r in range(1, NZ):
        in_ninth(r).wait_recv()
    for r in (3, 5, 1, 7):
        out_main(r).start()

    started = []

    def send(src, rsem, device):
        copy = remote(src, src, send_b.at[len(started)], rsem, device)
        copy.start()
        started.append(copy)

    def block(xx, yy):
        return (yy * 4 + xx) * 2 + c

    def whole(b, h, device):
        send(rows.at[b, h, 0 : PART[h]], recv_b.at[2 * b + h], device)

    def arrived(b, h):
        remote(rows.at[b, h, 0 : PART[h]], rows.at[b, h, 0 : PART[h]], send_b.at[0], recv_b.at[2 * b + h], sibling).wait_recv()

    mine = block(x, yp)
    other = block(x, 1 - yp)
    cut = (slice(0, 1792), slice(1792, WIDE))

    def compute(yy, xx, hs=(0, 1)):
        u = yy * 4 + xx
        n = len(hs)
        at = slice(hs[0], hs[-1] + 1)
        for h in hs:
            arrived(2 * u + 1 - c, h)
        tok = rows[pl.ds(2 * u, 2), at, :, 0:D].reshape(2 * n * HROWS, D)
        grad = rows[pl.ds(2 * u, 2), at, :, D:TWO].reshape(2 * n * HROWS, D)
        pre = dot(tok, win_in[...])
        cdf = 0.5 * (1.0 + lax.erf(pre * (1.0 / math.sqrt(2.0))))
        density = jnp.exp(-0.5 * pre * pre) * (1.0 / math.sqrt(2.0 * math.pi))
        act = (pre * cdf).astype(BF)
        gpre = (dot(grad, wout_in[...], LAST) * (cdf + pre * density)).astype(BF)
        part[pl.ds(2 * u, 2), at, :, 0:D] = dot(act, wout_in[...]).astype(BF).reshape(2, n, HROWS, D)
        part[pl.ds(2 * u, 2), at, :, D:TWO] = dot(gpre, win_in[...], LAST).astype(BF).reshape(2, n, HROWS, D)
        act_all[u, :, at] = act.reshape(2, n, HROWS, HID)
        gpre_all[u, :, at] = gpre.reshape(2, n, HROWS, HID)
        for h in hs:
            core_copy(u, h).start()

    def core_copy(u, h):
        k = 2 * u + h
        return remote(part.at[2 * u + 1 - c, h, 0 : PART[h]], tot.at[u, h, 0 : PART[h]], send_c.at[k], recv_c.at[k], sibling)

    def merge(yy, xx, h):
        u = yy * 4 + xx
        core_copy(u, h).wait_recv()
        n = PART[h]
        tot[u, h, 0:n] = tot[u, h, 0:n] + part[2 * u + c, h, 0:n]

    def cross_copy(h):
        return remote(tot.at[(1 - yp) * 4 + xo, h, 0 : PART[h]], cross.at[h, 0 : PART[h]], send_x.at[h], recv_x.at[h], across)

    def half_copy(s, h):
        piece = tot.at[yp * 4 + xo, h, 0 : PART[h], s * D : (s + 1) * D]
        k = 2 * s + h
        return remote(piece, halves.at[k, 0 : PART[h]], send_hf.at[k], recv_hf.at[k], right if s == 0 else left)

    def full_copy(o, s, h):
        u = (yp if o == 0 else 1 - yp) * 4 + (xr if s == 0 else xl)
        k = (2 * o + s) * 2 + h
        return remote(tot.at[u, h, 0 : PART[h]], full.at[k, 0 : PART[h]], send_f.at[k], recv_f.at[k], right if s == 0 else left)

    def y_copy(h):
        return remote(ysum.at[h, 0 : PART[h]], yrecv.at[h, 0 : PART[h]], send_y.at[h], recv_y.at[h], across)

    def own_rows(h):
        rows[mine, h, 0:32, :] = landing[4 * h : 4 * h + 4].reshape(4 * BASE, WIDE)
        if h == 0:
            for i in range(NZ):
                both = landx[i].astype(F32)
                ninths[i : i + 1, 0:D] = both[0:1, 0:D]
                ninths[i : i + 1, D:TWO] = both[1:2, 0:D]
                ninths[i : i + 1, TWO:WIDE] = both[0:1, D:PAIR]
            rows[mine, h, 32:40, :] = ninths[0:NZ, :].astype(BF)
        for device in (across, right, left, sibling):
            whole(mine, h, device)

    def from_row(h):
        b = block(xl, yp)
        arrived(b, h)
        send(rows.at[b, h, 0 : PART[h], cut[0]], recv_h.at[2 * h], right)
        whole(b, h, sibling)
        b = block(xr, yp)
        arrived(b, h)
        send(rows.at[b, h, 0 : PART[h], cut[1]], recv_h.at[2 * h + 1], left)
        whole(b, h, sibling)

    def from_across(h):
        arrived(other, h)
        for device in (right, left, sibling):
            whole(other, h, device)

    def from_far(h):
        b = block(xo, yp)
        for s in range(2):
            piece = rows.at[b, h, 0 : PART[h], cut[s]]
            remote(piece, piece, send_b.at[0], recv_h.at[2 * h + s], sibling).wait_recv()
        whole(b, h, across)
        whole(b, h, sibling)

    def from_other_row(xx, h):
        b = block(xx, 1 - yp)
        arrived(b, h)
        whole(b, h, sibling)

    own_rows(0)
    from_row(0)
    from_across(0)
    for r in (1, 3, 5, 7):
        in_main(r).wait_recv()
    own_rows(1)
    weights_in.wait()
    weights_out.wait()
    from_far(0)
    for yy, xx in ((yp, x), (1 - yp, x), (yp, xl), (yp, xr)):
        compute(yy, xx, (0,))
    from_row(1)
    from_across(1)
    compute(yp, xo, (0,))
    compute(yp, x, (1,))
    compute(1 - yp, x, (1,))
    from_far(1)
    compute(yp, xl, (1,))
    compute(yp, xr, (1,))
    for h in range(2):
        from_other_row(xl, h)
        from_other_row(xr, h)
    compute(1 - yp, xr)
    compute(1 - yp, xl)
    from_other_row(xo, 0)
    compute(1 - yp, xo, (0,))
    for h in range(2):
        for s in range(2):
            merge(1 - yp, xl if s else xr, h)
            full_copy(1, s, h).start()
    compute(yp, xo, (1,))
    merge(1 - yp, xo, 0)
    cross_copy(0).start()
    from_other_row(xo, 1)
    compute(1 - yp, xo, (1,))
    for h in range(2):
        merge(yp, xo, h)
    merge(1 - yp, xo, 1)
    cross_copy(1).start()
    for h in range(2):
        merge(yp, xr, h)
        merge(yp, xl, h)
    for h in range(2):
        merge(1 - yp, x, h)
        merge(yp, x, h)

    level = lane[0:1, :].astype(F32)
    above = jnp.zeros((1, 128), F32)
    for u in range(8):
        key = rows[2 * u : 2 * u + 2, :, :, TWO:WIDE].reshape(4 * HROWS, 128).astype(F32)
        above = above + jnp.sum((key > level).astype(F32), axis=0, keepdims=True)
    cutoff = jnp.sum((above > CAP).astype(F32), axis=1, keepdims=True)
    for u in range(8):
        key = rows[2 * u : 2 * u + 2, :, :, TWO:WIDE].reshape(4 * HROWS, 128).astype(F32)
        keep_all[u] = (key > cutoff).astype(BF)
    keep_own = [(rows[mine, h, 0 : PART[h], TWO : TWO + 1].astype(F32) > cutoff).astype(F32) for h in range(2)]

    for u in range(8):
        keep = jnp.concatenate([keep_all[u], keep_all[u]], axis=1).reshape(2, 2, HROWS, HID)
        act_all[u] = act_all[u] * keep
        gpre_all[u] = gpre_all[u] * keep

    def out_gradients(lo, hi):
        @pl.loop(lo, hi)
        def _(i):
            at = pl.multiple_of(i * 128, 128)
            g = rows[:, :, :, pl.ds(D + at, 128)].reshape(32 * HROWS, 128)
            gout[:, pl.ds(at, 128)] = dot(act_all[...].reshape(32 * HROWS, HID), g, FIRST).astype(BF)

    def in_gradients(lo, hi):
        @pl.loop(lo, hi)
        def _(i):
            at = pl.multiple_of(i * 128, 128)
            t = rows[:, :, :, pl.ds(at, 128)].reshape(32 * HROWS, 128)
            gin[pl.ds(at, 128), :] = dot(t, gpre_all[...].reshape(32 * HROWS, HID), FIRST).astype(BF)

    def cross_step(h):
        cross_copy(h).wait_recv()
        n = PART[h]
        tot[yp * 4 + xo, h, 0:n] = tot[yp * 4 + xo, h, 0:n] + cross[h, 0:n]
        half_copy(0, h).start()
        half_copy(1, h).start()

    def half_step(h):
        for s in range(2):
            half_copy(s, h).wait_recv()
            u = yp * 4 + (xr if s == 0 else xl)
            lanes = slice(s * D, (s + 1) * D)
            n = PART[h]
            tot[u, h, 0:n, lanes] = tot[u, h, 0:n, lanes] + halves[2 * s + h, 0:n]
            full_copy(0, s, h).start()

    def y_step(h):
        full_copy(1, 0, h).wait_recv()
        full_copy(1, 1, h).wait_recv()
        n = PART[h]
        total = tot[(1 - yp) * 4 + x, h, 0:n].astype(F32) + full[4 + h, 0:n].astype(F32) + full[6 + h, 0:n].astype(F32)
        ysum[h, 0:n] = total.astype(BF)
        y_copy(h).start()

    cross_step(0)
    y_step(0)
    half_step(0)
    cross_step(1)
    y_step(1)
    out_gradients(0, 5)
    half_step(1)

    def home_main(r):
        k = seat((NZ - r) % NZ)
        return remote(spread.at[seat(r)], back.at[k], send_e.at[r], recv_e.at[k], sources[r])

    def home_ninth(r):
        k = seat((NZ - r) % NZ)
        return remote(spreadx.at[seat(r)], backx.at[k], send_ex.at[r], recv_ex.at[k], sources[r])

    def home_wait(r):
        k = seat(r)
        remote(back.at[k], back.at[k], send_e.at[0], recv_e.at[k], targets[r]).wait_recv()

    def ninth_wait(r):
        k = seat(r)
        remote(backx.at[k], backx.at[k], send_ex.at[0], recv_ex.at[k], targets[r]).wait_recv()

    for h in range(2):
        y_copy(h).wait_recv()
        n = PART[h]
        total = tot[yp * 4 + x, h, 0:n].astype(F32) + yrecv[h, 0:n].astype(F32)
        for s in range(2):
            full_copy(0, s, h).wait_recv()
            total = total + full[2 * s + h, 0:n].astype(F32)
        final = (total * keep_own[h]).astype(BF)
        spread[4 * h : 4 * h + 4] = final[0:32].reshape(4, BASE, TWO)
        if h == 0:
            single = final[32:40].astype(F32)
            for i in range(NZ):
                spreadx[i] = jnp.concatenate([single[i : i + 1, 0:D], single[i : i + 1, D:TWO]], axis=0).astype(BF)
        for r in (4 + h, 2 + h, 6 + h):
            home_main(r).start()
        if h:
            home_main(1).start()
        else:

            @pl.when(jnp.logical_not(own))
            def _():
                home_main(0).start()
                home_ninth(0).start()

            for r in (4, 3, 5, 2, 6, 1, 7):
                home_ninth(r).start()
            out_gradients(5, 10)

            @pl.when(own)
            def _():
                local(
                    (
                        (spread.at[0], back.at[0], send_e.at[0]),
                        (spreadx.at[0], backx.at[0], send_ex.at[0]),
                    )
                )

    out_gradients(10, 13)
    gradients_out = pltpu.make_async_copy(gout, gout_ref, local_sem.at[2])
    gradients_out.start()
    in_gradients(0, 4)

    def tail(src, dst, ssem, rsem):
        return [remote(src(n, to), dst(n), ssem.at[n - 1], rsem.at[n - 1], (dp, to)) for n, to in ((2, xo), (3, xr), (1, xl))]

    tails = []
    parts = (slice(0, 48), slice(48, PLACES))

    def result_part(p):
        for k in range(2):
            value = result[parts[p], k * D : (k + 1) * D]
            for i in range(4):
                chunk[i, k, parts[p], :] = value[:, i * OUTW : (i + 1) * OUTW]
        copies = tail(
            lambda n, to: chunk.at[to, :, parts[p]], lambda n: gathered.at[n, :, parts[p]], send_o.at[p], recv_o.at[p]
        )
        for copy in copies:
            copy.start()
        tails.extend(copies)

    for r in (4, 2, 6):
        home_wait(r)

    @pl.when(jnp.logical_not(own))
    def _():
        home_wait(0)
        ninth_wait(0)

    for r in range(1, NZ):
        ninth_wait(r)
    for r in range(NZ):
        both = backx[r].astype(F32)
        ninths[r : r + 1, 0:D] = both[0:1]
        ninths[r : r + 1, D:TWO] = both[1:2]
    result[0:32, :] = back[0:4].reshape(4 * BASE, TWO)
    result[32:48, :] = ninths[:, 0:TWO].astype(BF)
    result_part(0)
    in_gradients(4, 13)
    gradients_in = pltpu.make_async_copy(gin, gin_ref, local_sem.at[3])
    gradients_in.start()
    for r in (1, 3, 5, 7):
        home_wait(r)
    result[48:PLACES, :] = back[4:8].reshape(4 * BASE, TWO)
    result_part(1)
    cot = cot16.astype(F32)
    value = result[:, 0:D]
    gg0 = jnp.sum(cot * dot(seats[0, 0:PLACES], value, FIRST), axis=1, keepdims=True)
    gg1 = jnp.sum(cot * dot(seats[1, 0:PLACES], value, FIRST), axis=1, keepdims=True)
    gg[...] = jnp.where(lane == 0, gg0, jnp.where(lane == 1, gg1, 0.0)).reshape(4, 32, 128)
    last = tail(lambda n, to: gg.at[to], lambda n: gg_in.at[n - 1], send_g, recv_g)
    for copy in last:
        copy.start()
    gathered[0] = chunk[x]
    tails.extend(last)
    for copy in tails:
        copy.wait_recv()
    gates = gg[x]
    for n in range(3):
        gates = gates + gg_in[n]
    gg_ref[...] = gates[:, 0:2]
    outs = gathered[:, 0].reshape(4 * PLACES, OUTW)
    mixed = gate_ref[0:1, :] * dot(outs, seats[0], FIRST) + gate_ref[1:2, :] * dot(outs, seats[1], FIRST)
    out_ref[...] = mixed.astype(BF)
    moved = gathered[:, 1].reshape(4 * PLACES, OUTW)
    dx_ref[...] = dot(moved, seats[0] + seats[1], FIRST).astype(BF)

    gradients_out.wait()
    gradients_in.wait()

    def sent(r):
        for copy in (out_main(r), out_ninth(r), home_main(r), home_ninth(r)):
            copy.wait_send()

    for r in range(1, NZ):
        sent(r)

    @pl.when(jnp.logical_not(own))
    def _():
        sent(0)

    for copy in started + tails:
        copy.wait_send()
    for u in range(8):
        for h in range(2):
            core_copy(u, h).wait_send()
    for h in range(2):
        cross_copy(h).wait_send()
        y_copy(h).wait_send()
        for s in range(2):
            half_copy(s, h).wait_send()
            full_copy(0, s, h).wait_send()
            full_copy(1, s, h).wait_send()


def layer(*args):
    dma = pltpu.SemaphoreType.DMA
    vmem = pltpu.VMEM
    return pl.pallas_call(
        layer_kernel,
        out_shape=(
            jax.ShapeDtypeStruct((OUTW, 128), BF),
            jax.ShapeDtypeStruct((OUTW, 128), BF),
            jax.ShapeDtypeStruct((32, 2), F32),
            jax.ShapeDtypeStruct((D, HID), BF),
            jax.ShapeDtypeStruct((HID, D), BF),
        ),
        in_specs=[pl.BlockSpec(memory_space=vmem)] * 5
        + [pl.BlockSpec(memory_space=pl.ANY)] * 2,
        out_specs=[pl.BlockSpec(memory_space=vmem)] * 3 + [pl.BlockSpec(memory_space=pl.ANY)] * 2,
        scratch_shapes=[
            vmem((NZ, BASE, WIDE), BF),
            vmem((NZ, 2, PAIR), BF),
            vmem((NZ, BASE, WIDE), BF),
            vmem((NZ, 2, PAIR), BF),
            vmem((16, 2, HROWS, WIDE), BF),
            vmem((16, 2, HROWS, TWO), BF),
            vmem((8, 2, HROWS, TWO), BF),
            vmem((2, HROWS, TWO), BF),
            vmem((4, HROWS, D), BF),
            vmem((8, HROWS, TWO), BF),
            vmem((2, HROWS, TWO), BF),
            vmem((2, HROWS, TWO), BF),
            vmem((NZ, BASE, TWO), BF),
            vmem((NZ, 2, D), BF),
            vmem((NZ, BASE, TWO), BF),
            vmem((NZ, 2, D), BF),
            vmem((16, WIDE), F32),
            vmem((PLACES, TWO), BF),
            vmem((4, 2, PLACES, OUTW), BF),
            vmem((4, 2, PLACES, OUTW), BF),
            vmem((4, 32, 128), F32),
            vmem((3, 32, 128), F32),
            vmem((2, 4 * PLACES, 128), BF),
            vmem((D, HID), BF),
            vmem((HID, D), BF),
            vmem((D, HID), BF),
            vmem((HID, D), BF),
            vmem((8, 2, 2, HROWS, HID), BF),
            vmem((8, 2, 2, HROWS, HID), BF),
            vmem((8, 4 * HROWS, 128), BF),
            dma((8,)), dma((8,)), dma((8,)), dma((8,)), dma((32,)), dma((32,)), dma((4,)),
            dma((16,)), dma((16,)), dma((2,)), dma((2,)), dma((4,)), dma((4,)),
            dma((8,)), dma((8,)), dma((2,)), dma((2,)), dma((8,)), dma((8,)), dma((8,)), dma((8,)),
            dma((2, 3)), dma((2, 3)), dma((3,)), dma((3,)), dma((4,)),
        ],
        compiler_params=pltpu.CompilerParams(collective_id=0, has_side_effects=True, vmem_limit_bytes=VMEM_LIMIT),
        name="layer",
    )(*args)


def body(tokens, expert_ids, priority, gate_values, weight_in, weight_out, cotangent):
    mixed, token_grad, gate_grad, grad_in, grad_out = layer(
        expert_ids.T, priority[None, :], gate_values.T, tokens, cotangent, weight_in[0], weight_out[0],
    )
    return mixed.T, token_grad.T, gate_grad, grad_in[None], grad_out[None]


def solution(mesh):
    placed = (
        P("dp", None),
        P("dp", None),
        P("dp"),
        P("dp", None),
        P("dp", None, "rep"),
        P("dp", "rep", None),
        P("dp", None),
    )
    return jax.shard_map(
        body,
        mesh=mesh,
        in_specs=placed,
        out_specs=(
            P("dp", "rep"),
            P("dp", "rep"),
            P(("dp", "rep"), None),
            P("dp", None, "rep"),
            P("dp", "rep", None),
        ),
        check_vma=False,
    )
```
